32 devices in a mesh: group: 2 (over y), inst: 4 (over x, core), brick: 4 (over z).
Axes of the slice: x: 2, y: 2, z: 4, core: 2. Of those that a mesh axis runs over, the one named last changes fastest.
Arguments:
- state: float32 [32, 5, 32, 4096], P(('group', 'inst'), None, 'brick'), parts along dimension 0, may hold values from -1.5 to 4, as said below
- time_step: float32 [64, 4096], P(('group', 'brick')), parts along dimension 0, may hold values from 0.05 to 0.5
- blocks: bfloat16 [8, 320, 320], replicated, may hold values from -0.3125 to 0.3125
- cut_counts: int32 [8], P('group'), parts along dimension 0, may hold values from 1 to 256, 384 in all
- tile_index: int32 [8, 256], P(('group', 'brick')), parts along dimension 0, may hold values from 0 to 511, as said below
- tile_type: int32 [8, 256], P(('group', 'brick')), parts along dimension 0, may hold values from 0 to 7
Outputs:
- residual: float32 [32, 5, 32, 4096], P(('group', 'inst'), None, 'brick'), parts along dimension 0
- new_state: float32 [32, 5, 32, 4096], P(('group', 'inst'), None, 'brick'), parts along dimension 0
The draws below stay inside these ranges and needn't reach their ends.
There are 2 independent parts, one for each index of `group`. The reference program is written for one: setup_inputs(seed, part) draws one part's arguments, and reference() takes and returns one part's arrays. A program takes and returns all parts, laid end to end along the dimension named above; an argument that names none is the same for every part. Nothing has to cross between parts.
Inputs may be any that keep to these rules, and one draw needn't show every extreme that they name: `state`: component 0 (density) lies in 0.5 to 2, components 1 to 3 in -1.5 to 1.5, component 4 in 1.5 to 4. `tile_index`: row b lists 256 different tiles of brick b. `cut_counts`: the entries sum to 384.
All inputs are finite; a program needn't handle non-finite values.
Results may differ from the reference program's by a relative error of at most 0.0013.
Values may be sent and summed in bfloat16 or wider, within the bound.
No kernel may reach another device: no remote copies, remote signals or barrier semaphores. Data moves between devices by JAX's collectives and lax.ppermute only.
A program may use at most 64 MiB of HBM per device.

```python
import math
import jax
import jax.numpy as jnp
import numpy as np
from jax import lax

NINST = 16
NVAR = 5
TILE = 64
KTYPES = 8
CS = 4096
NX = 32
TSIZE = 320
TILES_DEV = 512
TCAP = 256
CUT_MEAN = 96
N_BRICK = 4


def draw_state(key, part):
    shape = (NINST, NX, CS)
    key_one, key_two, key_three = jax.random.split(key, 3)
    density = jax.random.uniform(key_one, shape, jnp.float32, 0.5, 2.0)
    energy = jax.random.uniform(key_three, shape, jnp.float32, 1.5, 4.0)
    momentum = jnp.clip(0.5 * jax.random.normal(key_two, (3,) + shape, jnp.float32), -1.5, 1.5)
    return jnp.concatenate([density[:, None], jnp.transpose(momentum, (1, 0, 2, 3)), energy[:, None]], axis=1)


def draw_tile_index(key, part):
    keys = jax.random.split(key, N_BRICK + 1)
    where_to = jax.random.randint(keys[N_BRICK], (), 0, TCAP)

    def one_row(row_key, row):
        order = jax.random.permutation(row_key, TILES_DEV).astype(jnp.int32)
        found = jnp.argmax(order == TILES_DEV - 1).astype(jnp.int32)
        moved = jnp.roll(order, where_to - found)
        chosen = jnp.where(row == 0, moved, order)
        return chosen[:TCAP]
    return jax.vmap(one_row)(keys[:N_BRICK], jnp.arange(N_BRICK, dtype=jnp.int32))


def plant(entries, key, low, high):
    place = [jax.random.randint(jax.random.fold_in(key, axis), (), 0, length) for axis, length in enumerate(entries.shape)]
    longest = entries.shape.index(max(entries.shape))
    neighbour = place[:longest] + [(place[longest] + 1) % entries.shape[longest]] + place[longest + 1:]
    return entries.at[tuple(place)].set(low).at[tuple(neighbour)].set(high)


def block_levels(key, shape, pieces, least, high):
    def one(axis_at, blocks):
        heights = jax.random.uniform(jax.random.fold_in(jax.random.fold_in(key, 6), axis_at), (blocks,), jnp.float32, least / len(pieces), high / len(pieces))
        return jnp.repeat(jnp.exp(heights), shape[axis_at] // blocks).reshape((-1,) + (1,) * (len(shape) - axis_at - 1))

    loudness = one(*pieces[0])
    for cut in pieces[1:]:
        loudness = loudness * one(*cut)
    return loudness


def length_profile(number_of, total, bound, slope):
    loads = [(1 << 20) // math.isqrt(grade ** slope) + 1 for grade in range(2, number_of + 1)]
    spare, counts = total - bound - (number_of - 1), [1] * (number_of - 1)
    while spare > 0:
        candidates = [i for i in range(number_of - 1) if counts[i] < bound]
        whole, left = sum([loads[i] for i in candidates]), spare
        for i in candidates:
            extra = min(bound - counts[i], max(1, left * loads[i] // whole), spare)
            counts[i] = counts[i] + extra
            spare = spare - extra
    return np.array([bound] + counts)


def uneven(rng, count, total, bound, lean):
    if count == 2:
        one = jax.random.randint(rng, (), max(1, total - bound), min(bound, total - 1) + 1)
        return jnp.stack([one, total - one])
    tallies = jnp.asarray(length_profile(count, total, bound, lean), jnp.int32)
    couples = (count - 1) // 2
    giver, receiver = tallies[1:1 + 2 * couples:2], tallies[2:2 + 2 * couples:2]
    margin = jnp.minimum(giver - 1, bound - receiver)
    moved = jax.random.randint(jax.random.fold_in(rng, 1), (couples,), 0, 1 << 20) % (margin + 1)
    tallies = tallies.at[1:1 + 2 * couples:2].set(giver - moved).at[2:2 + 2 * couples:2].set(receiver + moved)
    return tallies[jax.random.permutation(jax.random.fold_in(rng, 2), count)]


def centred(rng, extent, deviation, bound, kind=jnp.bfloat16):
    array = deviation * jax.random.normal(rng, extent, jnp.float32)
    return jnp.clip(array, min=-bound, max=bound).astype(kind)


def setup_inputs(seed: int = 0, part: int = 0) -> dict:
    streams_of = jax.random.split(jax.random.key(seed), 7)
    own_keys = jax.random.split(jax.random.fold_in(streams_of[6], part), 7)
    state = draw_state(jax.random.fold_in(jax.random.fold_in(streams_of[6], part), 71), part)
    time_step = jnp.clip(jnp.exp(math.log(0.5) - 2.3025851 * jax.random.uniform(own_keys[1], (NX, CS), jnp.float32) ** block_levels(own_keys[1], (NX, CS), ((0, 4),), -0.2, 0.2)), 0.05, 0.5)
    blocks = centred(streams_of[2], (KTYPES, TSIZE, TSIZE), TSIZE ** -0.5, 0.3125)
    cut_counts = uneven(own_keys[3], N_BRICK, N_BRICK * CUT_MEAN, TCAP, 2).astype(jnp.int32)
    tile_index = draw_tile_index(jax.random.fold_in(jax.random.fold_in(streams_of[6], part), 71), part)
    tile_type = plant(jax.random.randint(own_keys[5], (N_BRICK, TCAP), 0, KTYPES), jax.random.fold_in(own_keys[5], 1), 0, KTYPES - 1).astype(jnp.int32)
    return dict(state=state, time_step=time_step, blocks=blocks, cut_counts=cut_counts, tile_index=tile_index, tile_type=tile_type)


GAMMA_MINUS = 0.4
EPS_FOURTH = 0.03125


def spectral_entry(diff, count):
    shifted = jnp.mod(diff, count)
    sign = 1.0 - 2.0 * jnp.mod(diff, 2).astype(jnp.float32)
    safe = jnp.where(shifted == 0, 1, shifted).astype(jnp.float32)
    value = sign / jnp.tan(jnp.pi * safe / count)
    return jnp.where(shifted == 0, 0.0, value).astype(jnp.float32)


def euler_flux(state):
    density = state[:, 0]
    mom_one = state[:, 1]
    mom_two = state[:, 2]
    mom_three = state[:, 3]
    energy = state[:, 4]
    speed = mom_one / density
    press = GAMMA_MINUS * (energy - 0.5 * (mom_one * mom_one + mom_two * mom_two + mom_three * mom_three) / density)
    return jnp.stack([mom_one, mom_one * speed + press, mom_two * speed, mom_three * speed, (energy + press) * speed], axis=1)


def reference(state, time_step, blocks, cut_counts, tile_index, tile_type):
    flux = euler_flux(state)
    wide = jnp.pad(jnp.concatenate([flux, state], axis=1), ((0, 0), (0, 0), (2, 2), (0, 0)))
    fpad = wide[:, :NVAR]
    qpad = wide[:, NVAR:]
    transport = 0.5 * (fpad[:, :, 3:-1] - fpad[:, :, 1:-3])
    smoothing = EPS_FOURTH * (qpad[:, :, 4:] - 4.0 * qpad[:, :, 3:-1] + 6.0 * qpad[:, :, 2:-2] - 4.0 * qpad[:, :, 1:-3] + qpad[:, :, :-4])
    every = jnp.arange(NINST, dtype=jnp.int32)
    dmat = spectral_entry(every[:, None] - every[None, :], NINST)
    timewise = jnp.einsum('jk,kcxs->jcxs', dmat, state, precision=lax.Precision.HIGHEST)
    tiles = state.reshape(NINST, NVAR, N_BRICK, TILES_DEV, TILE).transpose(2, 3, 0, 1, 4).reshape(N_BRICK, TILES_DEV, NINST, TSIZE)
    slots = jnp.arange(TCAP, dtype=jnp.int32)

    def one_brick(inputs):
        brick_tiles, index_row, type_row, count = inputs
        chosen = brick_tiles[index_row].astype(jnp.bfloat16)
        kinds = blocks[type_row]
        prod = jnp.einsum('tab,tib->tia', kinds.astype(jnp.float32), chosen.astype(jnp.float32), precision=lax.Precision.HIGHEST)
        prod = jnp.where((slots < count)[:, None, None], prod, 0.0)
        return jnp.zeros((TILES_DEV, NINST, TSIZE), jnp.float32).at[index_row].add(prod)

    cut_tiles = lax.map(one_brick, (tiles, tile_index, tile_type, cut_counts))
    cut = cut_tiles.reshape(N_BRICK, TILES_DEV, NINST, NVAR, TILE).transpose(2, 3, 0, 1, 4).reshape(NINST, NVAR, NX, CS)
    residual = transport + smoothing + cut + timewise
    new_state = state - time_step[None, None] * residual
    return residual, new_state
```

```python
import functools
import math

import jax
import jax.numpy as jnp
from jax import lax
from jax.experimental import pallas as pl
from jax.experimental.pallas import tpu as pltpu
from jax.sharding import PartitionSpec as P

TILE = 64
GAMMA_MINUS = 0.4
EPS_FOURTH = 0.03125
LANES = 128
MIB = 1 << 20
CENTRE = (1.25, 0.0, 0.0, 0.0, 2.75)
STATE_VARS = (1, 2)
SUM_GROUPS = ((3, 4), (0,))

IN_VMEM = pl.BlockSpec(memory_space=pltpu.VMEM)
IN_HBM = pl.BlockSpec(memory_space=pltpu.HBM)
IN_SMEM = pl.BlockSpec(memory_space=pltpu.SMEM)


def params(mib):
    return pltpu.CompilerParams(vmem_limit_bytes=mib * MIB)


def spectral(m, period):
    m = m % period
    if m == 0:
        return 0.0
    return (-1.0) ** m / math.tan(math.pi * m / period)


def row_coefs(j, inst, period, base, parity):
    own = [spectral(base * inst + j - k, period) for k in range(inst)]
    even = [spectral((base - 1) * inst + j - k, period) for k in range(inst)]
    odd = [spectral((base + 1) * inst + j - k, period) for k in range(inst)]
    mate = [jnp.where(parity == 0, jnp.float32(a), jnp.float32(b)) for a, b in zip(even, odd)]
    return own + mate


def weighted(coefs, values):
    total = None
    for c, x in zip(coefs, values):
        if isinstance(c, float) and c == 0.0:
            continue
        total = c * x if total is None else total + c * x
    return total


def centred(x, v):
    return x - CENTRE[v] if CENTRE[v] else x


def columns(cells, width, body):
    def one(c, carry):
        body(pl.ds(pl.multiple_of(c * width, width), width), c)
        return carry

    lax.fori_loop(0, cells // width, one, 0)


def pack_state_kernel(state_ref, out_ref, held_ref, sems):
    inst, _, _, cells = state_ref.shape
    chunks = sems.shape[0]
    width = cells // chunks
    lo, hi = STATE_VARS[0], STATE_VARS[-1] + 1
    copies = []
    for c in range(chunks):
        cols = pl.ds(c * width, width)
        copies.append(pltpu.make_async_copy(state_ref.at[:, lo:hi, :, cols], held_ref.at[:, :, :, cols], sems.at[c]))
        copies[-1].start()
    for c in range(chunks):
        copies[c].wait()

        def body(cols, _, base=c * width):
            at = pl.ds(pl.multiple_of(base + cols.start, LANES), LANES)
            for n, v in enumerate(STATE_VARS):
                packed = jnp.concatenate([centred(held_ref[k, n, :, at], v) for k in range(inst)], axis=0)
                out_ref[n, :, at] = packed.astype(jnp.bfloat16)

        columns(width, LANES, body)


def pack_state(state, chunks=2):
    inst, _, rows, cells = state.shape
    n = len(STATE_VARS)
    return pl.pallas_call(
        pack_state_kernel,
        in_specs=[IN_HBM],
        out_specs=IN_VMEM,
        out_shape=pltpu.VMEM((n, inst * rows, cells), jnp.bfloat16),
        scratch_shapes=[pltpu.VMEM((inst, n, rows, cells), jnp.float32), pltpu.SemaphoreType.DMA((chunks,))],
        compiler_params=params(4),
        name="pack_state",
    )(state)


def pack_edges_kernel(state_ref, held_ref, first_ref, second_ref, sems):
    inst, nvar, rows, cells = state_ref.shape
    chunks = sems.shape[0]
    width = cells // chunks
    odd = lax.axis_index("brick") % 2 == 1
    copies = []
    for c in range(chunks):
        cols = pl.ds(c * width, width)
        copies.append(pltpu.make_async_copy(state_ref.at[:, :, :, cols], held_ref.at[:, :, :, cols], sems.at[c]))
        copies[-1].start()
    pair = lax.broadcasted_iota(jnp.int32, (rows, LANES), 0) // 2
    for c in range(chunks):
        copies[c].wait()

        def body(cols, _, base=c * width):
            at = pl.ds(pl.multiple_of(base + cols.start, LANES), LANES)
            for v in range(nvar):
                q = [held_ref[j, v, :, at] for j in range(inst)]
                head, tail = q[0], pltpu.roll(q[0], 2, 0)
                for j in range(1, inst):
                    head = jnp.where(pair == j, pltpu.roll(q[j], 2 * j, 0), head)
                    tail = jnp.where(pair == j, pltpu.roll(q[j], (2 * j + 2) % rows, 0) if (2 * j + 2) % rows else q[j], tail)
                first_ref[v, :, at] = jnp.where(odd, head, tail).astype(jnp.bfloat16)
                second_ref[v, :, at] = jnp.where(odd, tail, head).astype(jnp.bfloat16)

        columns(width, LANES, body)


def pack_edges(state, chunks=2):
    _, nvar, rows, cells = state.shape
    edge = pltpu.VMEM((nvar, rows, cells), jnp.bfloat16)
    return pl.pallas_call(
        pack_edges_kernel,
        in_specs=[IN_HBM],
        out_specs=[IN_VMEM] * 3,
        out_shape=[pltpu.VMEM(state.shape, jnp.float32), edge, edge],
        scratch_shapes=[pltpu.SemaphoreType.DMA((chunks,))],
        compiler_params=params(4),
        name="pack_edges",
    )(state)


def send_sums_kernel(base, period, state_ref, mate_ref, *out_refs):
    inst, _, _, cells = state_ref.shape
    parity = lax.axis_index("inst") % 2
    coefs = [row_coefs(j, inst, period, base, parity) for j in range(inst)]

    def body(cols, _):
        for group, out_ref in zip(SUM_GROUPS, out_refs):
            for n, v in enumerate(group):
                values = [centred(ref[k, v, :, cols], v) for ref in (state_ref, mate_ref) for k in range(inst)]
                sums = [weighted(coefs[j], values) for j in range(inst)]
                out_ref[n, :, cols] = jnp.concatenate(sums, axis=0).astype(jnp.bfloat16)

    columns(cells, LANES, body)


def send_sums(state, mate, base, period):
    inst, _, rows, cells = state.shape
    return pl.pallas_call(
        functools.partial(send_sums_kernel, base, period),
        in_specs=[IN_VMEM] * 2,
        out_specs=[IN_VMEM] * len(SUM_GROUPS),
        out_shape=[pltpu.VMEM((len(g), inst * rows, cells), jnp.bfloat16) for g in SUM_GROUPS],
        compiler_params=params(4),
        name="send_sums",
    )(state, mate)


def expand_blocks(blocks_ref, wide_ref):
    kinds, size, _ = blocks_ref.shape
    nvar = size // TILE
    left = lax.broadcasted_iota(jnp.int32, (TILE, LANES), 1) < TILE
    for kind in range(kinds):
        for a in range(nvar):
            rows = pl.ds(a * TILE, TILE)
            for b in range(nvar):
                lo = (b // 2) * LANES
                hi = min(lo + LANES, size)
                piece = blocks_ref[kind, rows, lo:hi].astype(jnp.float32)
                if hi - lo < LANES:
                    piece = jnp.concatenate([piece, jnp.zeros_like(piece)], axis=1)
                turned = pltpu.roll(piece, TILE, 1)
                first, second = (piece, turned) if b % 2 == 0 else (turned, piece)
                at = pl.ds((kind * nvar + b) * LANES, LANES)
                wide_ref[pl.ds(a * LANES, TILE), at] = jnp.where(left, first, 0.0).astype(jnp.bfloat16)
                wide_ref[pl.ds(a * LANES + TILE, TILE), at] = jnp.where(left, 0.0, second).astype(jnp.bfloat16)


def tile_table(index_ref, type_ref, count, rows, per_row):
    slots = index_ref.shape[1]
    index = index_ref[...]
    slot = lax.broadcasted_iota(jnp.int32, (1, slots), 1)
    code = jnp.where(slot < count, type_ref[...] + 1, 0)
    row_of = lax.broadcasted_iota(jnp.int32, (rows, slots), 0)
    by_row = jnp.where(index // per_row == row_of, code, 0).astype(jnp.float32)
    col_of = lax.broadcasted_iota(jnp.int32, (per_row, slots), 0)
    by_col = jnp.where(index % per_row == col_of, 1.0, 0.0).astype(jnp.float32)
    return lax.dot_general(by_row, by_col, (((1,), (1,)), ((), ())), preferred_element_type=jnp.float32)


def cut_kernel(width, state_ref, blocks_ref, index_ref, type_ref, count_ref, out_ref, wide_ref, lhs_ref):
    inst, nvar, rows, cells = state_ref.shape
    kinds = blocks_ref.shape[0]
    per_row = cells // TILE
    per = inst * rows
    expand_blocks(blocks_ref, wide_ref)
    table = tile_table(index_ref, type_ref, count_ref[lax.axis_index("brick")], rows, per_row)

    def body(cols, chunk):
        tile_at = lax.broadcasted_iota(jnp.int32, (per_row, width), 0)
        cell_at = lax.broadcasted_iota(jnp.int32, (per_row, width), 1) + chunk * width
        spread = jnp.where(cell_at // TILE == tile_at, 1.0, 0.0).astype(jnp.float32)
        kind_map = jnp.dot(table, spread, preferred_element_type=jnp.float32)
        for c in range(width // LANES):
            at = pl.ds(pl.multiple_of(cols.start + c * LANES, LANES), LANES)
            here = kind_map[:, c * LANES:(c + 1) * LANES]
            here = jnp.concatenate([here] * inst, axis=0).astype(jnp.bfloat16)
            for v in range(nvar):
                packed = jnp.concatenate([state_ref[k, v, :, at] for k in range(inst)], axis=0).astype(jnp.bfloat16)
                for kind in range(kinds):
                    lhs_ref[pl.ds(c * per, per), pl.ds((kind * nvar + v) * LANES, LANES)] = jnp.where(
                        here == jnp.bfloat16(kind + 1.0), packed, jnp.bfloat16(0.0)
                    )
        prod = lax.dot_general(
            lhs_ref[...], wide_ref[...], (((1,), (1,)), ((), ())), preferred_element_type=jnp.float32
        )
        for c in range(width // LANES):
            at = pl.ds(pl.multiple_of(cols.start + c * LANES, LANES), LANES)
            for j in range(inst):
                for v in range(nvar):
                    r0 = c * per + j * rows
                    out_ref[j, v, :, at] = prod[r0:r0 + rows, v * LANES:(v + 1) * LANES]

    columns(cells, width, body)


def cut_terms(state, blocks, index, types, counts, width=1024):
    inst, _, rows, _ = state.shape
    kinds, size, _ = blocks.shape
    return pl.pallas_call(
        functools.partial(cut_kernel, width),
        in_specs=[IN_VMEM] * 4 + [IN_SMEM],
        out_specs=IN_VMEM,
        out_shape=pltpu.VMEM(state.shape, jnp.float32),
        scratch_shapes=[
            pltpu.VMEM((2 * size, 2 * size * kinds), jnp.bfloat16),
            pltpu.VMEM((width // LANES * inst * rows, 2 * size * kinds), jnp.bfloat16),
        ],
        compiler_params=params(16),
        name="cut_terms",
    )(state, blocks, index, types, counts)


def flux_of(q):
    inv = 1.0 / jnp.where(q[0] == 0.0, 1.0, q[0])
    speed = q[1] * inv
    press = GAMMA_MINUS * (q[4] - 0.5 * (q[1] * q[1] + q[2] * q[2] + q[3] * q[3]) * inv)
    return [q[1], q[1] * speed + press, q[2] * speed, q[3] * speed, (q[4] + press) * speed]


def turn(x, shift):
    shift = shift % x.shape[0]
    return pltpu.roll(x, shift, 0) if shift else x


def stencil_kernel(period, state_ref, mate_ref, cut_ref, first_ref, second_ref, out_ref):
    inst, nvar, rows, cells = state_ref.shape
    parity = lax.axis_index("inst") % 2
    odd = lax.axis_index("brick") % 2 == 1
    coefs = [row_coefs(j, inst, period, 0, parity) for j in range(inst)]
    row = lax.broadcasted_iota(jnp.int32, (rows, LANES), 0)

    def body(cols, _):
        times, above, below = [], [], []
        for v in range(nvar):
            values = [centred(ref[k, v, :, cols], v) for ref in (state_ref, mate_ref) for k in range(inst)]
            times.append([weighted(coefs[j], values) for j in range(inst)])
            first = first_ref[v, :, cols].astype(jnp.float32)
            second = second_ref[v, :, cols].astype(jnp.float32)
            above.append(jnp.where(odd, second, first))
            below.append(jnp.where(odd, first, second))
        for j in range(inst):
            up, down, smooth = [], [], []
            for v in range(nvar):
                x = state_ref[j, v, :, cols]
                h = jnp.where(row < rows // 2, turn(above[v], -2 * j), turn(below[v], rows - 2 - 2 * j))
                one = turn(jnp.where(row < 1, h, x), -1)
                two = turn(jnp.where(row < 2, h, x), -2)
                back = turn(jnp.where(row >= rows - 1, h, x), 1)
                back2 = turn(jnp.where(row >= rows - 2, h, x), 2)
                up.append(one)
                down.append(back)
                smooth.append(EPS_FOURTH * ((two + back2) - 4.0 * (one + back) + 6.0 * x))
            fup, fdown = flux_of(up), flux_of(down)
            for v in range(nvar):
                total = 0.5 * (fup[v] - fdown[v]) + smooth[v] + times[v][j]
                out_ref[j, v, :, cols] = total + cut_ref[j, v, :, cols]

    columns(cells, LANES, body)


def stencil(state, mate, cut, first, second, period):
    return pl.pallas_call(
        functools.partial(stencil_kernel, period),
        in_specs=[IN_VMEM] * 5,
        out_specs=IN_VMEM,
        out_shape=pltpu.VMEM(state.shape, jnp.float32),
        compiler_params=params(4),
        name="stencil",
    )(state, mate, cut, first, second)


def finish_kernel(variables, sources, period, chunks, part_ref, state_ref, step_ref, *refs):
    inst, _, rows, cells = state_ref.shape
    got_refs = refs[:sources]
    res_ref, new_ref, res_held, new_held, sems = refs[-5:]
    parity = lax.axis_index("inst") % 2
    width = cells // chunks
    copies = []
    for c in range(chunks):
        for n, v in enumerate(variables):

            def body(cols, _, base=c * width, n=n, v=v):
                at = pl.ds(pl.multiple_of(base + cols.start, LANES), LANES)
                if v in STATE_VARS:
                    totals = [part_ref[j, v, :, at] for j in range(inst)]
                    for q in range(sources // 2):
                        coefs = [row_coefs(j, inst, period, 2 * (q + 1), parity) for j in range(inst)]
                        rows_of = [ref[n, :, at].astype(jnp.float32) for ref in got_refs[2 * q:2 * q + 2]]
                        values = [x[k * rows:(k + 1) * rows] for x in rows_of for k in range(inst)]
                        totals = [t + weighted(cf, values) for t, cf in zip(totals, coefs)]
                else:
                    got = [ref[n, :, at].astype(jnp.float32) for ref in got_refs]
                    totals = []
                    for j in range(inst):
                        total = part_ref[j, v, :, at]
                        for g in got:
                            total = total + g[j * rows:(j + 1) * rows]
                        totals.append(total)
                for j in range(inst):
                    res_held[j, n, :, at] = totals[j]
                    new_held[j, n, :, at] = state_ref[j, v, :, at] - step_ref[:, at] * totals[j]

            columns(width, LANES, body)
            cols = pl.ds(c * width, width)
            for held, out, which in ((res_held, res_ref, 0), (new_held, new_ref, 1)):
                copies.append(
                    pltpu.make_async_copy(held.at[:, n, :, cols], out.at[:, v, :, cols], sems.at[which, n, c])
                )
                copies[-1].start()
    for copy in copies:
        copy.wait()


def finish(variables, part, state, step, got, outs, period, chunks=2):
    inst, _, rows, cells = state.shape
    n = len(variables)
    operands = [part, state, step, *got]
    specs = [IN_VMEM] * len(operands)
    aliases = {}
    if outs is not None:
        aliases = {len(operands): 0, len(operands) + 1: 1}
        operands += list(outs)
        specs += [IN_HBM] * 2
    return pl.pallas_call(
        functools.partial(finish_kernel, variables, len(got), period, chunks),
        in_specs=specs,
        out_specs=[IN_HBM] * 2,
        out_shape=[jax.ShapeDtypeStruct(state.shape, jnp.float32)] * 2,
        scratch_shapes=[
            pltpu.VMEM((inst, n, rows, cells), jnp.float32),
            pltpu.VMEM((inst, n, rows, cells), jnp.float32),
            pltpu.SemaphoreType.DMA((2, n, chunks)),
        ],
        input_output_aliases=aliases,
        compiler_params=params(6),
        name="finish",
    )(*operands)


def section(state, time_step, blocks, cut_counts, tile_index, tile_type):
    inst = state.shape[0]
    groups = lax.axis_size("inst")
    bricks = lax.axis_size("brick")
    period = inst * groups
    swap = [(i, i ^ 1) for i in range(groups)]
    hops = [[(i, (i + 2 * q) % groups) for i in range(groups)] for q in range(1, groups // 2)]
    state = pltpu.with_memory_space_constraint(state, pltpu.HBM)

    packed = pack_state(state)
    got_state = [lax.ppermute(packed, "inst", hop) for hop in hops]
    mate = pltpu.with_memory_space_constraint(lax.ppermute(state, "inst", swap), pltpu.VMEM)
    held, first, second = pack_edges(state)
    evens = [(b, b + 1) for b in range(0, bricks - 1, 2)]
    odds = [(b, b + 1) for b in range(1, bricks - 1, 2)]
    first = lax.ppermute(first, "brick", evens + [(b, a) for a, b in evens])
    second = lax.ppermute(second, "brick", odds + [(b, a) for a, b in odds])
    got_sums = [[] for _ in SUM_GROUPS]
    for q, hop in enumerate(hops):
        for g, part in enumerate(send_sums(held, mate, 2 * (q + 1), period)):
            got_sums[g].append(lax.ppermute(part, "inst", hop))
    cut = cut_terms(held, blocks, tile_index, tile_type, cut_counts)
    part = stencil(held, mate, cut, first, second, period)
    pairs = []
    for got in got_state:
        pairs += [got, lax.ppermute(got, "inst", swap)]
    outs = finish(STATE_VARS, part, held, time_step, pairs, None, period)
    for g, group in enumerate(SUM_GROUPS):
        outs = finish(group, part, held, time_step, got_sums[g], outs, period)
    return tuple(outs)


def solution(mesh):
    placed = (
        P(("group", "inst"), None, "brick", None),
        P(("group", "brick"), None),
        P(),
        P("group"),
        P(("group", "brick"), None),
        P(("group", "brick"), None),
    )
    return jax.shard_map(
        section,
        mesh=mesh,
        in_specs=placed,
        out_specs=(
            P(("group", "inst"), None, "brick", None),
            P(("group", "inst"), None, "brick", None),
        ),
        check_vma=False,
    )
```

```python
import functools
import math

import jax
import jax.numpy as jnp
from jax import lax
from jax.experimental import pallas as pl
from jax.experimental.pallas import tpu as pltpu
from jax.sharding import PartitionSpec as P

TILE = 64
GAMMA_MINUS = 0.4
EPS_FOURTH = 0.03125
LANES = 128
UNROLL = 2
MIB = 1 << 20
CENTRE = (1.25, 0.0, 0.0, 0.0, 2.75)
STATE_VARS = (1, 2)
SUM_GROUPS = ((3, 4), (0,))

IN_VMEM = pl.BlockSpec(memory_space=pltpu.VMEM)
IN_HBM = pl.BlockSpec(memory_space=pltpu.HBM)
IN_SMEM = pl.BlockSpec(memory_space=pltpu.SMEM)


def params(mib):
    return pltpu.CompilerParams(vmem_limit_bytes=mib * MIB)


def spectral(m, period):
    m = m % period
    if m == 0:
        return 0.0
    return (-1.0) ** m / math.tan(math.pi * m / period)


def row_coefs(j, inst, period, base, parity):
    own = [spectral(base * inst + j - k, period) for k in range(inst)]
    even = [spectral((base - 1) * inst + j - k, period) for k in range(inst)]
    odd = [spectral((base + 1) * inst + j - k, period) for k in range(inst)]
    mate = [jnp.where(parity == 0, jnp.float32(a), jnp.float32(b)) for a, b in zip(even, odd)]
    return own + mate


def weighted(coefs, values):
    total = None
    for c, x in zip(coefs, values):
        if isinstance(c, float) and c == 0.0:
            continue
        total = c * x if total is None else total + c * x
    return total


def centred(x, v):
    return x - CENTRE[v] if CENTRE[v] else x


def columns(cells, width, body):
    def one(c, carry):
        body(pl.ds(pl.multiple_of(c * width, width), width), c)
        return carry

    lax.fori_loop(0, cells // width, one, 0)


def pack_state_kernel(state_ref, out_ref, held_ref, sems):
    inst, _, _, cells = state_ref.shape
    chunks = sems.shape[0]
    width = cells // chunks
    lo, hi = STATE_VARS[0], STATE_VARS[-1] + 1
    copies = []
    for c in range(chunks):
        cols = pl.ds(c * width, width)
        copies.append(pltpu.make_async_copy(state_ref.at[:, lo:hi, :, cols], held_ref.at[:, :, :, cols], sems.at[c]))
        copies[-1].start()
    for c in range(chunks):
        copies[c].wait()

        def body(cols, _, base=c * width):
            at = pl.ds(pl.multiple_of(base + cols.start, LANES), LANES)
            for n, v in enumerate(STATE_VARS):
                packed = jnp.concatenate([centred(held_ref[k, n, :, at], v) for k in range(inst)], axis=0)
                out_ref[n, :, at] = packed.astype(jnp.bfloat16)

        columns(width, LANES, body)


def pack_state(state, chunks=4):
    inst, _, rows, cells = state.shape
    n = len(STATE_VARS)
    return pl.pallas_call(
        pack_state_kernel,
        in_specs=[IN_HBM],
        out_specs=IN_VMEM,
        out_shape=pltpu.VMEM((n, inst * rows, cells), jnp.bfloat16),
        scratch_shapes=[pltpu.VMEM((inst, n, rows, cells), jnp.float32), pltpu.SemaphoreType.DMA((chunks,))],
        compiler_params=params(4),
        name="pack_state",
    )(state)


def pack_edges_kernel(state_ref, held_ref, first_ref, second_ref, sems):
    inst, nvar, rows, cells = state_ref.shape
    chunks = sems.shape[0]
    width = cells // chunks
    odd = lax.axis_index("brick") % 2 == 1
    copies = []
    for c in range(chunks):
        cols = pl.ds(c * width, width)
        copies.append(pltpu.make_async_copy(state_ref.at[:, :, :, cols], held_ref.at[:, :, :, cols], sems.at[c]))
        copies[-1].start()
    pair = lax.broadcasted_iota(jnp.int32, (rows, LANES), 0) // 2
    for c in range(chunks):
        copies[c].wait()

        def body(cols, _, base=c * width):
            at = pl.ds(pl.multiple_of(base + cols.start, LANES), LANES)
            for v in range(nvar):
                q = [held_ref[j, v, :, at] for j in range(inst)]
                head, tail = q[0], pltpu.roll(q[0], 2, 0)
                for j in range(1, inst):
                    head = jnp.where(pair == j, pltpu.roll(q[j], 2 * j, 0), head)
                    tail = jnp.where(pair == j, pltpu.roll(q[j], (2 * j + 2) % rows, 0) if (2 * j + 2) % rows else q[j], tail)
                first_ref[v, :, at] = jnp.where(odd, head, tail).astype(jnp.bfloat16)
                second_ref[v, :, at] = jnp.where(odd, tail, head).astype(jnp.bfloat16)

        columns(width, LANES, body)


def pack_edges(state, chunks=4):
    _, nvar, rows, cells = state.shape
    edge = pltpu.VMEM((nvar, rows, cells), jnp.bfloat16)
    return pl.pallas_call(
        pack_edges_kernel,
        in_specs=[IN_HBM],
        out_specs=[IN_VMEM] * 3,
        out_shape=[pltpu.VMEM(state.shape, jnp.float32), edge, edge],
        scratch_shapes=[pltpu.SemaphoreType.DMA((chunks,))],
        compiler_params=params(4),
        name="pack_edges",
    )(state)


def send_sums_kernel(base, period, state_ref, mate_ref, *out_refs):
    inst, _, _, cells = state_ref.shape
    parity = lax.axis_index("inst") % 2
    coefs = [row_coefs(j, inst, period, base, parity) for j in range(inst)]

    def body(cols, _):
        for group, out_ref in zip(SUM_GROUPS, out_refs):
            for n, v in enumerate(group):
                values = [centred(ref[k, v, :, cols], v) for ref in (state_ref, mate_ref) for k in range(inst)]
                sums = [weighted(coefs[j], values) for j in range(inst)]
                out_ref[n, :, cols] = jnp.concatenate(sums, axis=0).astype(jnp.bfloat16)

    columns(cells, LANES, body)


def send_sums(state, mate, base, period):
    inst, _, rows, cells = state.shape
    return pl.pallas_call(
        functools.partial(send_sums_kernel, base, period),
        in_specs=[IN_VMEM] * 2,
        out_specs=[IN_VMEM] * len(SUM_GROUPS),
        out_shape=[pltpu.VMEM((len(g), inst * rows, cells), jnp.bfloat16) for g in SUM_GROUPS],
        compiler_params=params(4),
        name="send_sums",
    )(state, mate)


def padded_size(size):
    return -(-size // LANES) * LANES


def cut_kernel(state_ref, blocks_ref, index_ref, type_ref, count_ref, out_ref, tiles_ref, wide_ref, lhs_ref, back_ref):
    inst, nvar, rows, cells = state_ref.shape
    kinds, size, _ = blocks_ref.shape
    slots = index_ref.shape[1]
    per_row = cells // TILE
    wide = padded_size(size)
    half = cells // LANES * rows
    left = lax.broadcasted_iota(jnp.int32, (2 * rows, LANES), 1) < TILE

    full = size // LANES * LANES
    for kind in range(kinds):
        wide_ref[0:size, kind * wide:kind * wide + full] = blocks_ref[kind, :, 0:full]
        rest = blocks_ref[kind, :, full:size]
        if size > full:
            blank = jnp.zeros((size, wide - size), jnp.bfloat16)
            wide_ref[0:size, kind * wide + full:(kind + 1) * wide] = jnp.concatenate([rest, blank], axis=1)
    if wide > size:
        wide_ref[size:wide, :] = jnp.zeros((wide - size, kinds * wide), jnp.bfloat16)

    def gather(cols, c):
        for i in range(inst):
            q = []
            for v in range(nvar):
                pair = [state_ref[i, v, :, pl.ds(pl.multiple_of(cols.start + n * LANES, LANES), LANES)] for n in range(2)]
                q.append(jnp.concatenate(pair, axis=0))
            turned = [pltpu.roll(x, TILE, 1) for x in q]
            for p in range(wide // LANES):
                u, w = 2 * p, 2 * p + 1
                lo = jnp.where(left, q[u], turned[w] if w < nvar else 0.0)
                hi = jnp.where(left, turned[u], q[w] if w < nvar else 0.0)
                at = pl.ds(i * wide + p * LANES, LANES)
                row = pl.multiple_of(c * 2 * rows, 2 * rows)
                tiles_ref[pl.ds(row, 2 * rows), at] = lo.astype(jnp.bfloat16)
                tiles_ref[pl.ds(half + row, 2 * rows), at] = hi.astype(jnp.bfloat16)

    columns(cells, 2 * LANES, gather)

    index = index_ref[...]
    used = lax.broadcasted_iota(jnp.int32, (1, slots), 1) < count_ref[lax.axis_index("brick")]
    place = index % 2 * half + index % per_row // 2 * rows + index // per_row
    place = jnp.where(used, place, -1)
    code = jnp.where(used, type_ref[...] + 1, 0)
    both = jnp.concatenate([place, code, jnp.zeros((6, slots), jnp.int32)], axis=0).astype(jnp.float32)
    upright = jnp.transpose(both)
    place_of = upright[:, 0:1].astype(jnp.int32)
    code_of = jnp.broadcast_to(upright[:, 1:2], (slots, LANES)).astype(jnp.bfloat16)
    pick = jnp.where(lax.broadcasted_iota(jnp.int32, (slots, 2 * half), 1) == place_of, 1.0, 0.0).astype(jnp.bfloat16)
    give = jnp.where(lax.broadcasted_iota(jnp.int32, (2 * half, slots), 0) == place, 1.0, 0.0).astype(jnp.bfloat16)

    chosen = jnp.dot(pick, tiles_ref[...], preferred_element_type=jnp.float32).astype(jnp.bfloat16)
    for kind in range(kinds):
        keep = code_of == jnp.bfloat16(kind + 1.0)
        for i in range(inst):
            for p in range(wide // LANES):
                piece = chosen[:, i * wide + p * LANES:i * wide + (p + 1) * LANES]
                at = pl.ds(kind * wide + p * LANES, LANES)
                lhs_ref[pl.ds(i * slots, slots), at] = jnp.where(keep, piece, jnp.bfloat16(0.0))
    prod = lax.dot_general(
        lhs_ref[...], wide_ref[...], (((1,), (1,)), ((), ())), preferred_element_type=jnp.float32
    )
    high = prod.astype(jnp.bfloat16)
    low = (prod - high.astype(jnp.float32)).astype(jnp.bfloat16)
    for i in range(inst):
        at = pl.ds(i * wide, wide)
        tiles_ref[0:slots, at] = high[i * slots:(i + 1) * slots]
        tiles_ref[slots:2 * slots, at] = low[i * slots:(i + 1) * slots]
    give = jnp.concatenate([give, give], axis=1)
    back_ref[...] = jnp.dot(give, tiles_ref[0:2 * slots, :], preferred_element_type=jnp.float32)

    def scatter(cols, c):
        row = pl.multiple_of(c * rows, rows)
        first = lax.broadcasted_iota(jnp.int32, (rows, LANES), 1) < TILE
        for i in range(inst):
            for v in range(nvar):
                at = pl.ds(i * wide + v // 2 * LANES, LANES)
                lo = back_ref[pl.ds(row, rows), at]
                hi = back_ref[pl.ds(half + row, rows), at]
                if v % 2 == 0:
                    hi = pltpu.roll(hi, TILE, 1)
                else:
                    lo = pltpu.roll(lo, TILE, 1)
                out_ref[i, v, :, cols] = jnp.where(first, lo, hi)

    columns(cells, LANES, scatter)


def cut_terms(state, blocks, index, types, counts):
    inst, _, rows, cells = state.shape
    kinds, size, _ = blocks.shape
    slots = index.shape[1]
    wide = padded_size(size)
    tiles = cells // TILE * rows
    return pl.pallas_call(
        cut_kernel,
        in_specs=[IN_VMEM] * 4 + [IN_SMEM],
        out_specs=IN_VMEM,
        out_shape=pltpu.VMEM(state.shape, jnp.float32),
        scratch_shapes=[
            pltpu.VMEM((max(tiles, 2 * slots), inst * wide), jnp.bfloat16),
            pltpu.VMEM((wide, kinds * wide), jnp.bfloat16),
            pltpu.VMEM((inst * slots, kinds * wide), jnp.bfloat16),
            pltpu.VMEM((tiles, inst * wide), jnp.float32),
        ],
        compiler_params=params(24),
        name="cut_terms",
    )(state, blocks, index, types, counts)


def flux_of(q):
    inv = 1.0 / jnp.where(q[0] == 0.0, 1.0, q[0])
    speed = q[1] * inv
    press = GAMMA_MINUS * (q[4] - 0.5 * (q[1] * q[1] + q[2] * q[2] + q[3] * q[3]) * inv)
    return [q[1], q[1] * speed + press, q[2] * speed, q[3] * speed, (q[4] + press) * speed]


def turn(x, shift):
    shift = shift % x.shape[0]
    return pltpu.roll(x, shift, 0) if shift else x


def stencil_kernel(period, state_ref, mate_ref, cut_ref, first_ref, second_ref, out_ref):
    inst, nvar, rows, cells = state_ref.shape
    parity = lax.axis_index("inst") % 2
    odd = lax.axis_index("brick") % 2 == 1
    coefs = [row_coefs(j, inst, period, 0, parity) for j in range(inst)]
    row = lax.broadcasted_iota(jnp.int32, (rows, LANES), 0)

    def body(cols, _):
        times, above, below = [], [], []
        for v in range(nvar):
            values = [centred(ref[k, v, :, cols], v) for ref in (state_ref, mate_ref) for k in range(inst)]
            times.append([weighted(coefs[j], values) for j in range(inst)])
            first = first_ref[v, :, cols].astype(jnp.float32)
            second = second_ref[v, :, cols].astype(jnp.float32)
            above.append(jnp.where(odd, second, first))
            below.append(jnp.where(odd, first, second))
        for j in range(inst):
            up, down, smooth = [], [], []
            for v in range(nvar):
                x = state_ref[j, v, :, cols]
                h = jnp.where(row < rows // 2, turn(above[v], -2 * j), turn(below[v], rows - 2 - 2 * j))
                one = turn(jnp.where(row < 1, h, x), -1)
                two = turn(jnp.where(row < 2, h, x), -2)
                back = turn(jnp.where(row >= rows - 1, h, x), 1)
                back2 = turn(jnp.where(row >= rows - 2, h, x), 2)
                up.append(one)
                down.append(back)
                smooth.append(EPS_FOURTH * ((two + back2) - 4.0 * (one + back) + 6.0 * x))
            fup, fdown = flux_of(up), flux_of(down)
            for v in range(nvar):
                total = 0.5 * (fup[v] - fdown[v]) + smooth[v] + times[v][j]
                out_ref[j, v, :, cols] = total + cut_ref[j, v, :, cols]

    columns(cells, LANES, body)


def stencil(state, mate, cut, first, second, period):
    return pl.pallas_call(
        functools.partial(stencil_kernel, period),
        in_specs=[IN_VMEM] * 5,
        out_specs=IN_VMEM,
        out_shape=pltpu.VMEM(state.shape, jnp.float32),
        compiler_params=params(4),
        name="stencil",
    )(state, mate, cut, first, second)


def finish_kernel(variables, sources, period, chunks, part_ref, state_ref, step_ref, *refs):
    inst, _, rows, cells = state_ref.shape
    got_refs = refs[:sources]
    res_ref, new_ref, res_held, new_held, sems = refs[-5:]
    parity = lax.axis_index("inst") % 2
    width = cells // chunks
    copies = []

    def one_column(n, v, at):
        if v in STATE_VARS:
            totals = [part_ref[j, v, :, at] for j in range(inst)]
            for q in range(sources // 2):
                coefs = [row_coefs(j, inst, period, 2 * (q + 1), parity) for j in range(inst)]
                rows_of = [ref[n, :, at].astype(jnp.float32) for ref in got_refs[2 * q:2 * q + 2]]
                values = [x[k * rows:(k + 1) * rows] for x in rows_of for k in range(inst)]
                totals = [t + weighted(cf, values) for t, cf in zip(totals, coefs)]
        else:
            got = [ref[n, :, at].astype(jnp.float32) for ref in got_refs]
            totals = []
            for j in range(inst):
                total = part_ref[j, v, :, at]
                for g in got:
                    total = total + g[j * rows:(j + 1) * rows]
                totals.append(total)
        for j in range(inst):
            res_held[j, n, :, at] = totals[j]
            new_held[j, n, :, at] = state_ref[j, v, :, at] - step_ref[:, at] * totals[j]

    for c in range(chunks):
        for n, v in enumerate(variables):

            def body(cols, _, base=c * width, n=n, v=v):
                for piece in range(UNROLL):
                    start = base + cols.start + piece * LANES
                    one_column(n, v, pl.ds(pl.multiple_of(start, LANES), LANES))

            columns(width, UNROLL * LANES, body)
            cols = pl.ds(c * width, width)
            for held, out, which in ((res_held, res_ref, 0), (new_held, new_ref, 1)):
                copies.append(
                    pltpu.make_async_copy(held.at[:, n, :, cols], out.at[:, v, :, cols], sems.at[which, n, c])
                )
                copies[-1].start()
    for copy in copies:
        copy.wait()


def finish(variables, part, state, step, got, outs, period, chunks=4):
    inst, _, rows, cells = state.shape
    n = len(variables)
    operands = [part, state, step, *got]
    specs = [IN_VMEM] * len(operands)
    aliases = {}
    if outs is not None:
        aliases = {len(operands): 0, len(operands) + 1: 1}
        operands += list(outs)
        specs += [IN_HBM] * 2
    return pl.pallas_call(
        functools.partial(finish_kernel, variables, len(got), period, chunks),
        in_specs=specs,
        out_specs=[IN_HBM] * 2,
        out_shape=[jax.ShapeDtypeStruct(state.shape, jnp.float32)] * 2,
        scratch_shapes=[
            pltpu.VMEM((inst, n, rows, cells), jnp.float32),
            pltpu.VMEM((inst, n, rows, cells), jnp.float32),
            pltpu.SemaphoreType.DMA((2, n, chunks)),
        ],
        input_output_aliases=aliases,
        compiler_params=params(6),
        name="finish",
    )(*operands)


def section(state, time_step, blocks, cut_counts, tile_index, tile_type):
    inst = state.shape[0]
    groups = lax.axis_size("inst")
    bricks = lax.axis_size("brick")
    period = inst * groups
    swap = [(i, i ^ 1) for i in range(groups)]
    hops = [[(i, (i + 2 * q) % groups) for i in range(groups)] for q in range(1, groups // 2)]
    state = pltpu.with_memory_space_constraint(state, pltpu.HBM)

    packed = pack_state(state)
    got_state = [lax.ppermute(packed, "inst", hop) for hop in hops]
    held, first, second = pack_edges(state)
    mate = pltpu.with_memory_space_constraint(lax.ppermute(held, "inst", swap), pltpu.VMEM)
    evens = [(b, b + 1) for b in range(0, bricks - 1, 2)]
    odds = [(b, b + 1) for b in range(1, bricks - 1, 2)]
    first = lax.ppermute(first, "brick", evens + [(b, a) for a, b in evens])
    second = lax.ppermute(second, "brick", odds + [(b, a) for a, b in odds])
    got_sums = [[] for _ in SUM_GROUPS]
    for q, hop in enumerate(hops):
        for g, part in enumerate(send_sums(held, mate, 2 * (q + 1), period)):
            got_sums[g].append(lax.ppermute(part, "inst", hop))
    cut = cut_terms(held, blocks, tile_index, tile_type, cut_counts)
    part = stencil(held, mate, cut, first, second, period)
    pairs = []
    for got in got_state:
        pairs += [got, lax.ppermute(got, "inst", swap)]
    outs = finish(STATE_VARS, part, held, time_step, pairs, None, period)
    for g, group in enumerate(SUM_GROUPS):
        outs = finish(group, part, held, time_step, got_sums[g], outs, period)
    return tuple(outs)


def solution(mesh):
    placed = (
        P(("group", "inst"), None, "brick", None),
        P(("group", "brick"), None),
        P(),
        P("group"),
        P(("group", "brick"), None),
        P(("group", "brick"), None),
    )
    return jax.shard_map(
        section,
        mesh=mesh,
        in_specs=placed,
        out_specs=(
            P(("group", "inst"), None, "brick", None),
            P(("group", "inst"), None, "brick", None),
        ),
        check_vma=False,
    )
```

```python
import functools
import math

import jax
import jax.numpy as jnp
from jax import lax
from jax.experimental import pallas as pl
from jax.experimental.pallas import tpu as pltpu
from jax.sharding import PartitionSpec as P

TILE = 64
GAMMA_MINUS = 0.4
EPS_FOURTH = 0.03125
LANES = 128
UNROLL = 2
MIB = 1 << 20
CENTRE = (1.25, 0.0, 0.0, 0.0, 2.75)
STATE_GROUPS = ((1, 2),)
PARTS = 2
SUM_GROUPS = (((3, 0, 2), (4, 0, 2), (0, 0, 1)), ((0, 1, 2),))

IN_VMEM = pl.BlockSpec(memory_space=pltpu.VMEM)
IN_HBM = pl.BlockSpec(memory_space=pltpu.HBM)
IN_SMEM = pl.BlockSpec(memory_space=pltpu.SMEM)


def params(mib):
    return pltpu.CompilerParams(vmem_limit_bytes=mib * MIB)


def spectral(m, period):
    m = m % period
    if m == 0:
        return 0.0
    return (-1.0) ** m / math.tan(math.pi * m / period)


def row_coefs(j, inst, period, base, parity):
    own = [spectral(base * inst + j - k, period) for k in range(inst)]
    even = [spectral((base - 1) * inst + j - k, period) for k in range(inst)]
    odd = [spectral((base + 1) * inst + j - k, period) for k in range(inst)]
    mate = [jnp.where(parity == 0, jnp.float32(a), jnp.float32(b)) for a, b in zip(even, odd)]
    return own + mate


def weighted(coefs, values):
    total = None
    for c, x in zip(coefs, values):
        if isinstance(c, float) and c == 0.0:
            continue
        total = c * x if total is None else total + c * x
    return total


def centred(x, v):
    return x - CENTRE[v] if CENTRE[v] else x


def columns(cells, width, body):
    def one(c, carry):
        body(pl.ds(pl.multiple_of(c * width, width), width), c)
        return carry

    lax.fori_loop(0, cells // width, one, 0)


def turn(x, shift):
    shift = shift % x.shape[0]
    return pltpu.roll(x, shift, 0) if shift else x


def pack_columns(refs_of, variables, inst, out_ref, base, cells):
    def body(cols, _):
        at = pl.ds(pl.multiple_of(base + cols.start, LANES), LANES)
        for n, v in enumerate(variables):
            packed = jnp.concatenate([centred(refs_of(k, n, at), v) for k in range(inst)], axis=0)
            out_ref[n, :, at] = packed.astype(jnp.bfloat16)

    columns(cells, LANES, body)


def pack_state_kernel(variables, state_ref, out_ref, held_ref, sems):
    inst, _, _, cells = state_ref.shape
    chunks = sems.shape[0]
    width = cells // chunks
    lo, hi = variables[0], variables[-1] + 1
    copies = []
    for c in range(chunks):
        cols = pl.ds(c * width, width)
        copies.append(pltpu.make_async_copy(state_ref.at[:, lo:hi, :, cols], held_ref.at[:, :, :, cols], sems.at[c]))
        copies[-1].start()
    for c in range(chunks):
        copies[c].wait()
        pack_columns(lambda k, n, at: held_ref[k, n, :, at], variables, inst, out_ref, c * width, width)


def pack_state(state, variables, chunks=4):
    inst, _, rows, cells = state.shape
    n = len(variables)
    return pl.pallas_call(
        functools.partial(pack_state_kernel, variables),
        in_specs=[IN_HBM],
        out_specs=IN_VMEM,
        out_shape=pltpu.VMEM((n, inst * rows, cells), jnp.bfloat16),
        scratch_shapes=[pltpu.VMEM((inst, n, rows, cells), jnp.float32), pltpu.SemaphoreType.DMA((chunks,))],
        compiler_params=params(4),
        name="pack_state",
    )(state)


def pack_more_kernel(variables, state_ref, out_ref):
    inst, _, _, cells = state_ref.shape
    pack_columns(lambda k, n, at: state_ref[k, variables[n], :, at], variables, inst, out_ref, 0, cells)


def pack_more(state, variables):
    inst, _, rows, cells = state.shape
    return pl.pallas_call(
        functools.partial(pack_more_kernel, variables),
        in_specs=[IN_VMEM],
        out_specs=IN_VMEM,
        out_shape=pltpu.VMEM((len(variables), inst * rows, cells), jnp.bfloat16),
        compiler_params=params(2),
        name="pack_more",
    )(state)


def pack_edges_kernel(state_ref, first_ref, second_ref):
    inst, nvar, rows, cells = state_ref.shape
    odd = lax.axis_index("brick") % 2 == 1
    pair = lax.broadcasted_iota(jnp.int32, (rows, LANES), 0) // 2

    def body(cols, _):
        for v in range(nvar):
            q = [state_ref[j, v, :, cols] for j in range(inst)]
            head, tail = q[0], turn(q[0], 2)
            for j in range(1, inst):
                head = jnp.where(pair == j, turn(q[j], 2 * j), head)
                tail = jnp.where(pair == j, turn(q[j], 2 * j + 2), tail)
            first_ref[v, :, cols] = jnp.where(odd, head, tail).astype(jnp.bfloat16)
            second_ref[v, :, cols] = jnp.where(odd, tail, head).astype(jnp.bfloat16)

    columns(cells, LANES, body)


def pack_edges(state):
    _, nvar, rows, cells = state.shape
    edge = pltpu.VMEM((nvar, rows, cells), jnp.bfloat16)
    return pl.pallas_call(
        pack_edges_kernel,
        in_specs=[IN_VMEM],
        out_specs=[IN_VMEM] * 2,
        out_shape=[edge, edge],
        compiler_params=params(2),
        name="pack_edges",
    )(state)


def laid_out(group, cells):
    pieces, at = [], 0
    for v, lo, hi in group:
        count = (hi - lo) * cells // PARTS
        pieces.append((v, lo * cells // PARTS, count, at))
        at += count
    return pieces, at


def send_sums_kernel(base, period, state_ref, mate_ref, *out_refs):
    inst, _, _, cells = state_ref.shape
    parity = lax.axis_index("inst") % 2
    coefs = [row_coefs(j, inst, period, base, parity) for j in range(inst)]
    for group, out_ref in zip(SUM_GROUPS, out_refs):
        for v, first, count, to in laid_out(group, cells)[0]:

            def body(cols, _, v=v, first=first, to=to, out_ref=out_ref):
                for piece in range(UNROLL):
                    start = cols.start + piece * LANES
                    src = pl.ds(pl.multiple_of(first + start, LANES), LANES)
                    dst = pl.ds(pl.multiple_of(to + start, LANES), LANES)
                    values = [centred(ref[k, v, :, src], v) for ref in (state_ref, mate_ref) for k in range(inst)]
                    sums = [weighted(coefs[j], values) for j in range(inst)]
                    out_ref[:, dst] = jnp.concatenate(sums, axis=0).astype(jnp.bfloat16)

            columns(count, UNROLL * LANES, body)


def send_sums(state, mate, base, period):
    inst, _, rows, cells = state.shape
    return pl.pallas_call(
        functools.partial(send_sums_kernel, base, period),
        in_specs=[IN_VMEM] * 2,
        out_specs=[IN_VMEM] * len(SUM_GROUPS),
        out_shape=[pltpu.VMEM((inst * rows, laid_out(g, cells)[1]), jnp.bfloat16) for g in SUM_GROUPS],
        compiler_params=params(4),
        name="send_sums",
    )(state, mate)


def padded_size(size):
    return -(-size // LANES) * LANES


def cut_kernel(state_ref, blocks_ref, index_ref, type_ref, count_ref, out_ref, tiles_ref, wide_ref, lhs_ref, back_ref):
    inst, nvar, rows, cells = state_ref.shape
    kinds, size, _ = blocks_ref.shape
    slots = index_ref.shape[1]
    per_row = cells // TILE
    wide = padded_size(size)
    half = cells // LANES * rows
    left = lax.broadcasted_iota(jnp.int32, (2 * rows, LANES), 1) < TILE

    full = size // LANES * LANES
    for kind in range(kinds):
        wide_ref[0:size, kind * wide:kind * wide + full] = blocks_ref[kind, :, 0:full]
        rest = blocks_ref[kind, :, full:size]
        if size > full:
            blank = jnp.zeros((size, wide - size), jnp.bfloat16)
            wide_ref[0:size, kind * wide + full:(kind + 1) * wide] = jnp.concatenate([rest, blank], axis=1)
    if wide > size:
        wide_ref[size:wide, :] = jnp.zeros((wide - size, kinds * wide), jnp.bfloat16)

    def gather(cols, c):
        for i in range(inst):
            q = []
            for v in range(nvar):
                pair = [state_ref[i, v, :, pl.ds(pl.multiple_of(cols.start + n * LANES, LANES), LANES)] for n in range(2)]
                q.append(jnp.concatenate(pair, axis=0))
            turned = [pltpu.roll(x, TILE, 1) for x in q]
            for p in range(wide // LANES):
                u, w = 2 * p, 2 * p + 1
                lo = jnp.where(left, q[u], turned[w] if w < nvar else 0.0)
                hi = jnp.where(left, turned[u], q[w] if w < nvar else 0.0)
                at = pl.ds(i * wide + p * LANES, LANES)
                row = pl.multiple_of(c * 2 * rows, 2 * rows)
                tiles_ref[pl.ds(row, 2 * rows), at] = lo.astype(jnp.bfloat16)
                tiles_ref[pl.ds(half + row, 2 * rows), at] = hi.astype(jnp.bfloat16)

    columns(cells, 2 * LANES, gather)

    index = index_ref[...]
    used = lax.broadcasted_iota(jnp.int32, (1, slots), 1) < count_ref[lax.axis_index("brick")]
    place = index % 2 * half + index % per_row // 2 * rows + index // per_row
    place = jnp.where(used, place, -1)
    code = jnp.where(used, type_ref[...] + 1, 0)
    both = jnp.concatenate([place, code, jnp.zeros((6, slots), jnp.int32)], axis=0).astype(jnp.float32)
    upright = jnp.transpose(both)
    place_of = upright[:, 0:1].astype(jnp.int32)
    code_of = jnp.broadcast_to(upright[:, 1:2], (slots, LANES)).astype(jnp.bfloat16)
    pick = jnp.where(lax.broadcasted_iota(jnp.int32, (slots, 2 * half), 1) == place_of, 1.0, 0.0).astype(jnp.bfloat16)
    give = jnp.where(lax.broadcasted_iota(jnp.int32, (2 * half, slots), 0) == place, 1.0, 0.0).astype(jnp.bfloat16)

    chosen = jnp.dot(pick, tiles_ref[...], preferred_element_type=jnp.float32).astype(jnp.bfloat16)
    for kind in range(kinds):
        keep = code_of == jnp.bfloat16(kind + 1.0)
        for i in range(inst):
            for p in range(wide // LANES):
                piece = chosen[:, i * wide + p * LANES:i * wide + (p + 1) * LANES]
                at = pl.ds(kind * wide + p * LANES, LANES)
                lhs_ref[pl.ds(i * slots, slots), at] = jnp.where(keep, piece, jnp.bfloat16(0.0))
    prod = lax.dot_general(
        lhs_ref[...], wide_ref[...], (((1,), (1,)), ((), ())), preferred_element_type=jnp.float32
    )
    high = prod.astype(jnp.bfloat16)
    low = (prod - high.astype(jnp.float32)).astype(jnp.bfloat16)
    for i in range(inst):
        at = pl.ds(i * wide, wide)
        tiles_ref[0:slots, at] = high[i * slots:(i + 1) * slots]
        tiles_ref[slots:2 * slots, at] = low[i * slots:(i + 1) * slots]
    give = jnp.concatenate([give, give], axis=1)
    back_ref[...] = jnp.dot(give, tiles_ref[0:2 * slots, :], preferred_element_type=jnp.float32)

    def scatter(cols, c):
        row = pl.multiple_of(c * rows, rows)
        first = lax.broadcasted_iota(jnp.int32, (rows, LANES), 1) < TILE
        for i in range(inst):
            for v in range(nvar):
                at = pl.ds(i * wide + v // 2 * LANES, LANES)
                lo = back_ref[pl.ds(row, rows), at]
                hi = back_ref[pl.ds(half + row, rows), at]
                if v % 2 == 0:
                    hi = pltpu.roll(hi, TILE, 1)
                else:
                    lo = pltpu.roll(lo, TILE, 1)
                out_ref[i, v, :, cols] = jnp.where(first, lo, hi)

    columns(cells, LANES, scatter)


def cut_terms(state, blocks, index, types, counts):
    inst, _, rows, cells = state.shape
    kinds, size, _ = blocks.shape
    slots = index.shape[1]
    wide = padded_size(size)
    tiles = cells // TILE * rows
    return pl.pallas_call(
        cut_kernel,
        in_specs=[IN_VMEM] * 4 + [IN_SMEM],
        out_specs=IN_VMEM,
        out_shape=pltpu.VMEM(state.shape, jnp.float32),
        scratch_shapes=[
            pltpu.VMEM((max(tiles, 2 * slots), inst * wide), jnp.bfloat16),
            pltpu.VMEM((wide, kinds * wide), jnp.bfloat16),
            pltpu.VMEM((inst * slots, kinds * wide), jnp.bfloat16),
            pltpu.VMEM((tiles, inst * wide), jnp.float32),
        ],
        compiler_params=params(24),
        name="cut_terms",
    )(state, blocks, index, types, counts)


def flux_of(q):
    inv = 1.0 / jnp.where(q[0] == 0.0, 1.0, q[0])
    speed = q[1] * inv
    press = GAMMA_MINUS * (q[4] - 0.5 * (q[1] * q[1] + q[2] * q[2] + q[3] * q[3]) * inv)
    return [q[1], q[1] * speed + press, q[2] * speed, q[3] * speed, (q[4] + press) * speed]


def stencil_kernel(period, state_ref, mate_ref, cut_ref, first_ref, second_ref, out_ref):
    inst, nvar, rows, cells = state_ref.shape
    parity = lax.axis_index("inst") % 2
    odd = lax.axis_index("brick") % 2 == 1
    coefs = [row_coefs(j, inst, period, 0, parity) for j in range(inst)]
    row = lax.broadcasted_iota(jnp.int32, (rows, LANES), 0)

    def body(cols, _):
        times, above, below = [], [], []
        for v in range(nvar):
            values = [centred(ref[k, v, :, cols], v) for ref in (state_ref, mate_ref) for k in range(inst)]
            times.append([weighted(coefs[j], values) for j in range(inst)])
            first = first_ref[v, :, cols].astype(jnp.float32)
            second = second_ref[v, :, cols].astype(jnp.float32)
            above.append(jnp.where(odd, second, first))
            below.append(jnp.where(odd, first, second))
        for j in range(inst):
            up, down, smooth = [], [], []
            for v in range(nvar):
                x = state_ref[j, v, :, cols]
                h = jnp.where(row < rows // 2, turn(above[v], -2 * j), turn(below[v], rows - 2 - 2 * j))
                one = turn(jnp.where(row < 1, h, x), -1)
                two = turn(jnp.where(row < 2, h, x), -2)
                back = turn(jnp.where(row >= rows - 1, h, x), 1)
                back2 = turn(jnp.where(row >= rows - 2, h, x), 2)
                up.append(one)
                down.append(back)
                smooth.append(EPS_FOURTH * ((two + back2) - 4.0 * (one + back) + 6.0 * x))
            fup, fdown = flux_of(up), flux_of(down)
            for v in range(nvar):
                total = 0.5 * (fup[v] - fdown[v]) + smooth[v] + times[v][j]
                out_ref[j, v, :, cols] = total + cut_ref[j, v, :, cols]

    columns(cells, LANES, body)


def stencil(state, mate, cut, first, second, period):
    return pl.pallas_call(
        functools.partial(stencil_kernel, period),
        in_specs=[IN_VMEM] * 5,
        out_specs=IN_VMEM,
        out_shape=pltpu.VMEM(state.shape, jnp.float32),
        compiler_params=params(4),
        name="stencil",
    )(state, mate, cut, first, second)


def finish_kernel(groups, period, part_ref, state_ref, step_ref, *refs):
    inst, _, rows, _ = state_ref.shape
    res_ref, new_ref, res_held, new_held, sems = refs[-5:]
    parity = lax.axis_index("inst") % 2
    jobs, at = [], 0
    for whole, pieces, count in groups:
        got_refs = refs[at:at + count]
        at += count
        jobs += [(whole, n, v, first, size, to, got_refs) for n, (v, first, size, to) in enumerate(pieces)]
    copies = []
    for m, (whole, n, v, first, size, to, got_refs) in enumerate(jobs):

        def one_column(start, m=m, whole=whole, n=n, v=v, first=first, to=to, got_refs=got_refs):
            at = pl.ds(pl.multiple_of(first + start, LANES), LANES)
            dst = pl.ds(pl.multiple_of(to + start, LANES), LANES)
            totals = [part_ref[j, v, :, at] for j in range(inst)]
            if whole:
                for q in range(len(got_refs) // 2):
                    coefs = [row_coefs(j, inst, period, 2 * (q + 1), parity) for j in range(inst)]
                    rows_of = [ref[n, :, at].astype(jnp.float32) for ref in got_refs[2 * q:2 * q + 2]]
                    values = [x[k * rows:(k + 1) * rows] for x in rows_of for k in range(inst)]
                    totals = [t + weighted(cf, values) for t, cf in zip(totals, coefs)]
            else:
                for ref in got_refs:
                    g = ref[:, dst].astype(jnp.float32)
                    totals = [t + g[j * rows:(j + 1) * rows] for j, t in enumerate(totals)]
            for j in range(inst):
                res_held[j, m, :, at] = totals[j]
                new_held[j, m, :, at] = state_ref[j, v, :, at] - step_ref[:, at] * totals[j]

        chunks = sems.shape[2]
        width = size // chunks
        for c in range(chunks):

            def body(cols, _, base=c * width, one_column=one_column):
                for piece in range(UNROLL):
                    one_column(base + cols.start + piece * LANES)

            columns(width, UNROLL * LANES, body)
            cols = pl.ds(first + c * width, width)
            for held, out, which in ((res_held, res_ref, 0), (new_held, new_ref, 1)):
                copies.append(
                    pltpu.make_async_copy(held.at[:, m, :, cols], out.at[:, v, :, cols], sems.at[which, m, c])
                )
                copies[-1].start()
    for copy in copies:
        copy.wait()


def finish(groups, part, state, step, outs, period, chunks=2):
    inst, _, rows, cells = state.shape
    n = sum(len(pieces) for _, pieces, _ in groups)
    operands = [part, state, step] + [x for _, _, got in groups for x in got]
    specs = [IN_VMEM] * len(operands)
    aliases = {}
    if outs is not None:
        aliases = {len(operands): 0, len(operands) + 1: 1}
        operands += list(outs)
        specs += [IN_HBM] * 2
    return pl.pallas_call(
        functools.partial(finish_kernel, [(w, p, len(got)) for w, p, got in groups], period),
        in_specs=specs,
        out_specs=[IN_HBM] * 2,
        out_shape=[jax.ShapeDtypeStruct(state.shape, jnp.float32)] * 2,
        scratch_shapes=[
            pltpu.VMEM((inst, n, rows, cells), jnp.float32),
            pltpu.VMEM((inst, n, rows, cells), jnp.float32),
            pltpu.SemaphoreType.DMA((2, n, chunks)),
        ],
        input_output_aliases=aliases,
        compiler_params=params(8),
        name="finish",
    )(*operands)


def section(state, time_step, blocks, cut_counts, tile_index, tile_type):
    inst = state.shape[0]
    groups = lax.axis_size("inst")
    bricks = lax.axis_size("brick")
    period = inst * groups
    swap = [(i, i ^ 1) for i in range(groups)]
    hops = [[(i, (i + 2 * q) % groups) for i in range(groups)] for q in range(1, groups // 2)]
    cells = state.shape[3]
    packed = [pack_state(pltpu.with_memory_space_constraint(state, pltpu.HBM), STATE_GROUPS[0])]
    held = pltpu.with_memory_space_constraint(state, pltpu.VMEM)
    packed += [pack_more(held, group) for group in STATE_GROUPS[1:]]
    got_state = [[lax.ppermute(p, "inst", hop) for hop in hops] for p in packed]
    first, second = pack_edges(held)
    mate = pltpu.with_memory_space_constraint(lax.ppermute(held, "inst", swap), pltpu.VMEM)
    evens = [(b, b + 1) for b in range(0, bricks - 1, 2)]
    odds = [(b, b + 1) for b in range(1, bricks - 1, 2)]
    first = lax.ppermute(first, "brick", evens + [(b, a) for a, b in evens])
    second = lax.ppermute(second, "brick", odds + [(b, a) for a, b in odds])
    got_sums = [[] for _ in SUM_GROUPS]
    for q, hop in enumerate(hops):
        for g, part in enumerate(send_sums(held, mate, 2 * (q + 1), period)):
            got_sums[g].append(lax.ppermute(part, "inst", hop))
    cut = cut_terms(held, blocks, tile_index, tile_type, cut_counts)
    part = stencil(held, mate, cut, first, second, period)
    groups = []
    for variables, got in zip(STATE_GROUPS, got_state):
        pairs = []
        for x in got:
            pairs += [x, lax.ppermute(x, "inst", swap)]
        groups.append((True, [(v, 0, cells, 0) for v in variables], pairs))
    steps = [groups]
    steps += [[(False, laid_out(group, cells)[0], got)] for group, got in zip(SUM_GROUPS, got_sums)]
    outs = None
    for step in steps:
        outs = finish(step, part, held, time_step, outs, period)
    return tuple(outs)


def solution(mesh):
    placed = (
        P(("group", "inst"), None, "brick", None),
        P(("group", "brick"), None),
        P(),
        P("group"),
        P(("group", "brick"), None),
        P(("group", "brick"), None),
    )
    return jax.shard_map(
        section,
        mesh=mesh,
        in_specs=placed,
        out_specs=(
            P(("group", "inst"), None, "brick", None),
            P(("group", "inst"), None, "brick", None),
        ),
        check_vma=False,
    )
```

```python
import functools
import math

import jax
import jax.numpy as jnp
from jax import lax
from jax.experimental import pallas as pl
from jax.experimental.pallas import tpu as pltpu
from jax.sharding import PartitionSpec as P

TILE = 64
GAMMA_MINUS = 0.4
EPS_FOURTH = 0.03125
LANES = 128
UNROLL = 2
MIB = 1 << 20
CENTRE = (1.25, 0.0, 0.0, 0.0, 2.75)
STATE_GROUPS = ((1, 2),)
PARTS = 2
SUM_GROUPS = (((3, 0, 2), (4, 0, 2), (0, 0, 1)), ((0, 1, 2),))

IN_VMEM = pl.BlockSpec(memory_space=pltpu.VMEM)
IN_HBM = pl.BlockSpec(memory_space=pltpu.HBM)
IN_SMEM = pl.BlockSpec(memory_space=pltpu.SMEM)


def params(mib):
    return pltpu.CompilerParams(vmem_limit_bytes=mib * MIB)


def spectral(m, period):
    m = m % period
    if m == 0:
        return 0.0
    return (-1.0) ** m / math.tan(math.pi * m / period)


def row_coefs(j, inst, period, base, parity):
    own = [spectral(base * inst + j - k, period) for k in range(inst)]
    even = [spectral((base - 1) * inst + j - k, period) for k in range(inst)]
    odd = [spectral((base + 1) * inst + j - k, period) for k in range(inst)]
    mate = [jnp.where(parity == 0, jnp.float32(a), jnp.float32(b)) for a, b in zip(even, odd)]
    return own + mate


def weighted(coefs, values):
    total = None
    for c, x in zip(coefs, values):
        if isinstance(c, float) and c == 0.0:
            continue
        total = c * x if total is None else total + c * x
    return total


def centred(x, v):
    return x - CENTRE[v] if CENTRE[v] else x


def columns(cells, width, body):
    def one(c, carry):
        body(pl.ds(pl.multiple_of(c * width, width), width), c)
        return carry

    lax.fori_loop(0, cells // width, one, 0)


def turn(x, shift):
    shift = shift % x.shape[0]
    return pltpu.roll(x, shift, 0) if shift else x


def pack_columns(refs_of, variables, inst, out_ref, base, cells):
    def body(cols, _):
        at = pl.ds(pl.multiple_of(base + cols.start, LANES), LANES)
        for n, v in enumerate(variables):
            packed = jnp.concatenate([centred(refs_of(k, n, at), v) for k in range(inst)], axis=0)
            out_ref[n, :, at] = packed.astype(jnp.bfloat16)

    columns(cells, LANES, body)


def pack_state_kernel(variables, state_ref, out_ref, held_ref, sems):
    inst, _, _, cells = state_ref.shape
    chunks = sems.shape[0]
    width = cells // chunks
    lo, hi = variables[0], variables[-1] + 1
    copies = []
    for c in range(chunks):
        cols = pl.ds(c * width, width)
        copies.append(pltpu.make_async_copy(state_ref.at[:, lo:hi, :, cols], held_ref.at[:, :, :, cols], sems.at[c]))
        copies[-1].start()
    for c in range(chunks):
        copies[c].wait()
        pack_columns(lambda k, n, at: held_ref[k, n, :, at], variables, inst, out_ref, c * width, width)


def pack_state(state, variables, chunks=4):
    inst, _, rows, cells = state.shape
    n = len(variables)
    return pl.pallas_call(
        functools.partial(pack_state_kernel, variables),
        in_specs=[IN_HBM],
        out_specs=IN_VMEM,
        out_shape=pltpu.VMEM((n, inst * rows, cells), jnp.bfloat16),
        scratch_shapes=[pltpu.VMEM((inst, n, rows, cells), jnp.float32), pltpu.SemaphoreType.DMA((chunks,))],
        compiler_params=params(4),
        name="pack_state",
    )(state)


def pack_more_kernel(variables, state_ref, out_ref):
    inst, _, _, cells = state_ref.shape
    pack_columns(lambda k, n, at: state_ref[k, variables[n], :, at], variables, inst, out_ref, 0, cells)


def pack_more(state, variables):
    inst, _, rows, cells = state.shape
    return pl.pallas_call(
        functools.partial(pack_more_kernel, variables),
        in_specs=[IN_VMEM],
        out_specs=IN_VMEM,
        out_shape=pltpu.VMEM((len(variables), inst * rows, cells), jnp.bfloat16),
        compiler_params=params(2),
        name="pack_more",
    )(state)


def pack_edges_kernel(state_ref, held_ref, first_ref, second_ref, sems):
    inst, nvar, rows, cells = state_ref.shape
    chunks = sems.shape[0]
    width = cells // chunks
    odd = lax.axis_index("brick") % 2 == 1
    copies = []
    for c in range(chunks):
        cols = pl.ds(c * width, width)
        copies.append(pltpu.make_async_copy(state_ref.at[:, :, :, cols], held_ref.at[:, :, :, cols], sems.at[c]))
        copies[-1].start()
    pair = lax.broadcasted_iota(jnp.int32, (rows, LANES), 0) // 2
    for c in range(chunks):
        copies[c].wait()

        def body(cols, _, base=c * width):
            at = pl.ds(pl.multiple_of(base + cols.start, LANES), LANES)
            for v in range(nvar):
                q = [held_ref[j, v, :, at] for j in range(inst)]
                head, tail = q[0], pltpu.roll(q[0], 2, 0)
                for j in range(1, inst):
                    head = jnp.where(pair == j, pltpu.roll(q[j], 2 * j, 0), head)
                    tail = jnp.where(pair == j, pltpu.roll(q[j], (2 * j + 2) % rows, 0) if (2 * j + 2) % rows else q[j], tail)
                first_ref[v, :, at] = jnp.where(odd, head, tail).astype(jnp.bfloat16)
                second_ref[v, :, at] = jnp.where(odd, tail, head).astype(jnp.bfloat16)

        columns(width, LANES, body)


def pack_edges(state, chunks=4):
    _, nvar, rows, cells = state.shape
    edge = pltpu.VMEM((nvar, rows, cells), jnp.bfloat16)
    return pl.pallas_call(
        pack_edges_kernel,
        in_specs=[IN_HBM],
        out_specs=[IN_VMEM] * 3,
        out_shape=[pltpu.VMEM(state.shape, jnp.float32), edge, edge],
        scratch_shapes=[pltpu.SemaphoreType.DMA((chunks,))],
        compiler_params=params(4),
        name="pack_edges",
    )(state)


def laid_out(group, cells):
    pieces, at = [], 0
    for v, lo, hi in group:
        count = (hi - lo) * cells // PARTS
        pieces.append((v, lo * cells // PARTS, count, at))
        at += count
    return pieces, at


def send_sums_kernel(base, period, state_ref, mate_ref, *out_refs):
    inst, _, _, cells = state_ref.shape
    parity = lax.axis_index("inst") % 2
    coefs = [row_coefs(j, inst, period, base, parity) for j in range(inst)]
    for group, out_ref in zip(SUM_GROUPS, out_refs):
        for v, first, count, to in laid_out(group, cells)[0]:

            def body(cols, _, v=v, first=first, to=to, out_ref=out_ref):
                for piece in range(UNROLL):
                    start = cols.start + piece * LANES
                    src = pl.ds(pl.multiple_of(first + start, LANES), LANES)
                    dst = pl.ds(pl.multiple_of(to + start, LANES), LANES)
                    values = [centred(ref[k, v, :, src], v) for ref in (state_ref, mate_ref) for k in range(inst)]
                    sums = [weighted(coefs[j], values) for j in range(inst)]
                    out_ref[:, dst] = jnp.concatenate(sums, axis=0).astype(jnp.bfloat16)

            columns(count, UNROLL * LANES, body)


def send_sums(state, mate, base, period):
    inst, _, rows, cells = state.shape
    return pl.pallas_call(
        functools.partial(send_sums_kernel, base, period),
        in_specs=[IN_VMEM] * 2,
        out_specs=[IN_VMEM] * len(SUM_GROUPS),
        out_shape=[pltpu.VMEM((inst * rows, laid_out(g, cells)[1]), jnp.bfloat16) for g in SUM_GROUPS],
        compiler_params=params(4),
        name="send_sums",
    )(state, mate)


def padded_size(size):
    return -(-size // LANES) * LANES


def cut_kernel(state_ref, blocks_ref, index_ref, type_ref, count_ref, out_ref, tiles_ref, wide_ref, lhs_ref, back_ref):
    inst, nvar, rows, cells = state_ref.shape
    kinds, size, _ = blocks_ref.shape
    slots = index_ref.shape[1]
    per_row = cells // TILE
    wide = padded_size(size)
    half = cells // LANES * rows
    left = lax.broadcasted_iota(jnp.int32, (2 * rows, LANES), 1) < TILE

    full = size // LANES * LANES
    for kind in range(kinds):
        wide_ref[0:size, kind * wide:kind * wide + full] = blocks_ref[kind, :, 0:full]
        rest = blocks_ref[kind, :, full:size]
        if size > full:
            blank = jnp.zeros((size, wide - size), jnp.bfloat16)
            wide_ref[0:size, kind * wide + full:(kind + 1) * wide] = jnp.concatenate([rest, blank], axis=1)
    if wide > size:
        wide_ref[size:wide, :] = jnp.zeros((wide - size, kinds * wide), jnp.bfloat16)

    def gather(cols, c):
        for i in range(inst):
            q = []
            for v in range(nvar):
                pair = [state_ref[i, v, :, pl.ds(pl.multiple_of(cols.start + n * LANES, LANES), LANES)] for n in range(2)]
                q.append(jnp.concatenate(pair, axis=0))
            turned = [pltpu.roll(x, TILE, 1) for x in q]
            for p in range(wide // LANES):
                u, w = 2 * p, 2 * p + 1
                lo = jnp.where(left, q[u], turned[w] if w < nvar else 0.0)
                hi = jnp.where(left, turned[u], q[w] if w < nvar else 0.0)
                at = pl.ds(i * wide + p * LANES, LANES)
                row = pl.multiple_of(c * 2 * rows, 2 * rows)
                tiles_ref[pl.ds(row, 2 * rows), at] = lo.astype(jnp.bfloat16)
                tiles_ref[pl.ds(half + row, 2 * rows), at] = hi.astype(jnp.bfloat16)

    columns(cells, 2 * LANES, gather)

    index = index_ref[...]
    used = lax.broadcasted_iota(jnp.int32, (1, slots), 1) < count_ref[lax.axis_index("brick")]
    place = index % 2 * half + index % per_row // 2 * rows + index // per_row
    place = jnp.where(used, place, -1)
    code = jnp.where(used, type_ref[...] + 1, 0)
    both = jnp.concatenate([place, code, jnp.zeros((6, slots), jnp.int32)], axis=0).astype(jnp.float32)
    upright = jnp.transpose(both)
    place_of = upright[:, 0:1].astype(jnp.int32)
    code_of = jnp.broadcast_to(upright[:, 1:2], (slots, LANES)).astype(jnp.bfloat16)
    pick = jnp.where(lax.broadcasted_iota(jnp.int32, (slots, 2 * half), 1) == place_of, 1.0, 0.0).astype(jnp.bfloat16)
    give = jnp.where(lax.broadcasted_iota(jnp.int32, (2 * half, slots), 0) == place, 1.0, 0.0).astype(jnp.bfloat16)

    chosen = jnp.dot(pick, tiles_ref[...], preferred_element_type=jnp.float32).astype(jnp.bfloat16)
    for kind in range(kinds):
        keep = code_of == jnp.bfloat16(kind + 1.0)
        for i in range(inst):
            for p in range(wide // LANES):
                piece = chosen[:, i * wide + p * LANES:i * wide + (p + 1) * LANES]
                at = pl.ds(kind * wide + p * LANES, LANES)
                lhs_ref[pl.ds(i * slots, slots), at] = jnp.where(keep, piece, jnp.bfloat16(0.0))
    prod = lax.dot_general(
        lhs_ref[...], wide_ref[...], (((1,), (1,)), ((), ())), preferred_element_type=jnp.float32
    )
    high = prod.astype(jnp.bfloat16)
    low = (prod - high.astype(jnp.float32)).astype(jnp.bfloat16)
    for i in range(inst):
        at = pl.ds(i * wide, wide)
        tiles_ref[0:slots, at] = high[i * slots:(i + 1) * slots]
        tiles_ref[slots:2 * slots, at] = low[i * slots:(i + 1) * slots]
    give = jnp.concatenate([give, give], axis=1)
    back_ref[...] = jnp.dot(give, tiles_ref[0:2 * slots, :], preferred_element_type=jnp.float32)

    def scatter(cols, c):
        row = pl.multiple_of(c * rows, rows)
        first = lax.broadcasted_iota(jnp.int32, (rows, LANES), 1) < TILE
        for i in range(inst):
            for v in range(nvar):
                at = pl.ds(i * wide + v // 2 * LANES, LANES)
                lo = back_ref[pl.ds(row, rows), at]
                hi = back_ref[pl.ds(half + row, rows), at]
                if v % 2 == 0:
                    hi = pltpu.roll(hi, TILE, 1)
                else:
                    lo = pltpu.roll(lo, TILE, 1)
                out_ref[i, v, :, cols] = jnp.where(first, lo, hi)

    columns(cells, LANES, scatter)


def cut_terms(state, blocks, index, types, counts):
    inst, _, rows, cells = state.shape
    kinds, size, _ = blocks.shape
    slots = index.shape[1]
    wide = padded_size(size)
    tiles = cells // TILE * rows
    return pl.pallas_call(
        cut_kernel,
        in_specs=[IN_VMEM] * 4 + [IN_SMEM],
        out_specs=IN_VMEM,
        out_shape=pltpu.VMEM(state.shape, jnp.float32),
        scratch_shapes=[
            pltpu.VMEM((max(tiles, 2 * slots), inst * wide), jnp.bfloat16),
            pltpu.VMEM((wide, kinds * wide), jnp.bfloat16),
            pltpu.VMEM((inst * slots, kinds * wide), jnp.bfloat16),
            pltpu.VMEM((tiles, inst * wide), jnp.float32),
        ],
        compiler_params=params(24),
        name="cut_terms",
    )(state, blocks, index, types, counts)


def flux_of(q):
    inv = 1.0 / jnp.where(q[0] == 0.0, 1.0, q[0])
    speed = q[1] * inv
    press = GAMMA_MINUS * (q[4] - 0.5 * (q[1] * q[1] + q[2] * q[2] + q[3] * q[3]) * inv)
    return [q[1], q[1] * speed + press, q[2] * speed, q[3] * speed, (q[4] + press) * speed]


def stencil_kernel(period, state_ref, mate_ref, cut_ref, first_ref, second_ref, out_ref):
    inst, nvar, rows, cells = state_ref.shape
    parity = lax.axis_index("inst") % 2
    odd = lax.axis_index("brick") % 2 == 1
    coefs = [row_coefs(j, inst, period, 0, parity) for j in range(inst)]
    shares = [sum(c) for c in coefs]
    row = lax.broadcasted_iota(jnp.int32, (rows, LANES), 0)

    def body(cols, _):
        above, below = [], []
        for v in range(nvar):
            first = first_ref[v, :, cols].astype(jnp.float32)
            second = second_ref[v, :, cols].astype(jnp.float32)
            above.append(jnp.where(odd, second, first))
            below.append(jnp.where(odd, first, second))
        for j in range(inst):
            up, down, smooth = [], [], []
            for v in range(nvar):
                x = state_ref[j, v, :, cols]
                h = jnp.where(row < rows // 2, turn(above[v], -2 * j), turn(below[v], rows - 2 - 2 * j))
                one = turn(jnp.where(row < 1, h, x), -1)
                two = turn(jnp.where(row < 2, h, x), -2)
                back = turn(jnp.where(row >= rows - 1, h, x), 1)
                back2 = turn(jnp.where(row >= rows - 2, h, x), 2)
                up.append(one)
                down.append(back)
                smooth.append(EPS_FOURTH * ((two + back2) - 4.0 * (one + back) + 6.0 * x))
            fup, fdown = flux_of(up), flux_of(down)
            for v in range(nvar):
                values = [ref[k, v, :, cols] for ref in (state_ref, mate_ref) for k in range(inst)]
                times = weighted(coefs[j], values)
                if CENTRE[v]:
                    times = times - CENTRE[v] * shares[j]
                total = 0.5 * (fup[v] - fdown[v]) + smooth[v] + times
                out_ref[j, v, :, cols] = total + cut_ref[j, v, :, cols]

    columns(cells, LANES, body)


def stencil(state, mate, cut, first, second, period):
    return pl.pallas_call(
        functools.partial(stencil_kernel, period),
        in_specs=[IN_VMEM] * 5,
        out_specs=IN_VMEM,
        out_shape=pltpu.VMEM(state.shape, jnp.float32),
        compiler_params=params(4),
        name="stencil",
    )(state, mate, cut, first, second)


def finish_kernel(groups, period, part_ref, state_ref, step_ref, *refs):
    inst, _, rows, _ = state_ref.shape
    res_ref, new_ref, res_held, new_held, sems = refs[-5:]
    parity = lax.axis_index("inst") % 2
    jobs, at = [], 0
    for whole, pieces, count in groups:
        got_refs = refs[at:at + count]
        at += count
        jobs += [(whole, n, v, first, size, to, got_refs) for n, (v, first, size, to) in enumerate(pieces)]
    copies = []
    for m, (whole, n, v, first, size, to, got_refs) in enumerate(jobs):

        def one_column(start, m=m, whole=whole, n=n, v=v, first=first, to=to, got_refs=got_refs):
            at = pl.ds(pl.multiple_of(first + start, LANES), LANES)
            dst = pl.ds(pl.multiple_of(to + start, LANES), LANES)
            totals = [part_ref[j, v, :, at] for j in range(inst)]
            if whole:
                for q in range(len(got_refs) // 2):
                    coefs = [row_coefs(j, inst, period, 2 * (q + 1), parity) for j in range(inst)]
                    rows_of = [ref[n, :, at].astype(jnp.float32) for ref in got_refs[2 * q:2 * q + 2]]
                    values = [x[k * rows:(k + 1) * rows] for x in rows_of for k in range(inst)]
                    totals = [t + weighted(cf, values) for t, cf in zip(totals, coefs)]
            else:
                for ref in got_refs:
                    g = ref[:, dst].astype(jnp.float32)
                    totals = [t + g[j * rows:(j + 1) * rows] for j, t in enumerate(totals)]
            for j in range(inst):
                res_held[j, m, :, at] = totals[j]
                new_held[j, m, :, at] = state_ref[j, v, :, at] - step_ref[:, at] * totals[j]

        chunks = sems.shape[2]
        width = size // chunks
        for c in range(chunks):

            def body(cols, _, base=c * width, one_column=one_column):
                for piece in range(UNROLL):
                    one_column(base + cols.start + piece * LANES)

            columns(width, UNROLL * LANES, body)
            cols = pl.ds(first + c * width, width)
            for held, out, which in ((res_held, res_ref, 0), (new_held, new_ref, 1)):
                copies.append(
                    pltpu.make_async_copy(held.at[:, m, :, cols], out.at[:, v, :, cols], sems.at[which, m, c])
                )
                copies[-1].start()
    for copy in copies:
        copy.wait()


def finish(groups, part, state, step, outs, period, chunks=2):
    inst, _, rows, cells = state.shape
    n = sum(len(pieces) for _, pieces, _ in groups)
    operands = [part, state, step] + [x for _, _, got in groups for x in got]
    specs = [IN_VMEM] * len(operands)
    aliases = {}
    if outs is not None:
        aliases = {len(operands): 0, len(operands) + 1: 1}
        operands += list(outs)
        specs += [IN_HBM] * 2
    return pl.pallas_call(
        functools.partial(finish_kernel, [(w, p, len(got)) for w, p, got in groups], period),
        in_specs=specs,
        out_specs=[IN_HBM] * 2,
        out_shape=[jax.ShapeDtypeStruct(state.shape, jnp.float32)] * 2,
        scratch_shapes=[
            pltpu.VMEM((inst, n, rows, cells), jnp.float32),
            pltpu.VMEM((inst, n, rows, cells), jnp.float32),
            pltpu.SemaphoreType.DMA((2, n, chunks)),
        ],
        input_output_aliases=aliases,
        compiler_params=params(8),
        name="finish",
    )(*operands)


def section(state, time_step, blocks, cut_counts, tile_index, tile_type):
    inst = state.shape[0]
    groups = lax.axis_size("inst")
    bricks = lax.axis_size("brick")
    period = inst * groups
    swap = [(i, i ^ 1) for i in range(groups)]
    hops = [[(i, (i + 2 * q) % groups) for i in range(groups)] for q in range(1, groups // 2)]
    cells = state.shape[3]
    state = pltpu.with_memory_space_constraint(state, pltpu.HBM)
    packed = [pack_state(state, STATE_GROUPS[0])]
    held, first, second = pack_edges(state)
    packed += [pack_more(held, group) for group in STATE_GROUPS[1:]]
    got_state = [[lax.ppermute(p, "inst", hop) for hop in hops] for p in packed]
    mate = pltpu.with_memory_space_constraint(lax.ppermute(held, "inst", swap), pltpu.VMEM)
    evens = [(b, b + 1) for b in range(0, bricks - 1, 2)]
    odds = [(b, b + 1) for b in range(1, bricks - 1, 2)]
    first = lax.ppermute(first, "brick", evens + [(b, a) for a, b in evens])
    second = lax.ppermute(second, "brick", odds + [(b, a) for a, b in odds])
    got_sums = [[] for _ in SUM_GROUPS]
    for q, hop in enumerate(hops):
        for g, part in enumerate(send_sums(held, mate, 2 * (q + 1), period)):
            got_sums[g].append(lax.ppermute(part, "inst", hop))
    cut = cut_terms(held, blocks, tile_index, tile_type, cut_counts)
    part = stencil(held, mate, cut, first, second, period)
    groups = []
    for variables, got in zip(STATE_GROUPS, got_state):
        pairs = []
        for x in got:
            pairs += [x, lax.ppermute(x, "inst", swap)]
        groups.append((True, [(v, 0, cells, 0) for v in variables], pairs))
    steps = [groups]
    steps += [[(False, laid_out(group, cells)[0], got)] for group, got in zip(SUM_GROUPS, got_sums)]
    outs = None
    for step in steps:
        outs = finish(step, part, held, time_step, outs, period)
    return tuple(outs)


def solution(mesh):
    placed = (
        P(("group", "inst"), None, "brick", None),
        P(("group", "brick"), None),
        P(),
        P("group"),
        P(("group", "brick"), None),
        P(("group", "brick"), None),
    )
    return jax.shard_map(
        section,
        mesh=mesh,
        in_specs=placed,
        out_specs=(
            P(("group", "inst"), None, "brick", None),
            P(("group", "inst"), None, "brick", None),
        ),
        check_vma=False,
    )
```

```python
import functools
import math

import jax
import jax.numpy as jnp
from jax import lax
from jax.experimental import pallas as pl
from jax.experimental.pallas import tpu as pltpu
from jax.sharding import PartitionSpec as P

TILE = 64
GAMMA_MINUS = 0.4
EPS_FOURTH = 0.03125
LANES = 128
UNROLL = 2
MIB = 1 << 20
CENTRE = (1.25, 0.0, 0.0, 0.0, 2.75)
STATE_GROUPS = ((1,), (2,))
PARTS = 2
SUM_GROUPS = (((3, 0, 2), (4, 0, 2), (0, 0, 1)), ((0, 1, 2),))

IN_VMEM = pl.BlockSpec(memory_space=pltpu.VMEM)
IN_HBM = pl.BlockSpec(memory_space=pltpu.HBM)
IN_SMEM = pl.BlockSpec(memory_space=pltpu.SMEM)


def params(mib):
    return pltpu.CompilerParams(vmem_limit_bytes=mib * MIB)


def spectral(m, period):
    m = m % period
    if m == 0:
        return 0.0
    return (-1.0) ** m / math.tan(math.pi * m / period)


def row_coefs(j, inst, period, base, parity):
    own = [spectral(base * inst + j - k, period) for k in range(inst)]
    even = [spectral((base - 1) * inst + j - k, period) for k in range(inst)]
    odd = [spectral((base + 1) * inst + j - k, period) for k in range(inst)]
    mate = [jnp.where(parity == 0, jnp.float32(a), jnp.float32(b)) for a, b in zip(even, odd)]
    return own + mate


def weighted(coefs, values):
    total = None
    for c, x in zip(coefs, values):
        if isinstance(c, float) and c == 0.0:
            continue
        total = c * x if total is None else total + c * x
    return total


def centred(x, v):
    return x - CENTRE[v] if CENTRE[v] else x


def columns(cells, width, body):
    def one(c, carry):
        body(pl.ds(pl.multiple_of(c * width, width), width), c)
        return carry

    lax.fori_loop(0, cells // width, one, 0)


def turn(x, shift):
    shift = shift % x.shape[0]
    return pltpu.roll(x, shift, 0) if shift else x


def pack_columns(refs_of, variables, inst, out_ref, base, cells):
    def body(cols, _):
        at = pl.ds(pl.multiple_of(base + cols.start, LANES), LANES)
        for n, v in enumerate(variables):
            packed = jnp.concatenate([centred(refs_of(k, n, at), v) for k in range(inst)], axis=0)
            out_ref[n, :, at] = packed.astype(jnp.bfloat16)

    columns(cells, LANES, body)


def pack_state_kernel(variables, state_ref, out_ref, held_ref, sems):
    inst, _, _, cells = state_ref.shape
    chunks = sems.shape[0]
    width = cells // chunks
    lo, hi = variables[0], variables[-1] + 1
    copies = []
    for c in range(chunks):
        cols = pl.ds(c * width, width)
        copies.append(pltpu.make_async_copy(state_ref.at[:, lo:hi, :, cols], held_ref.at[:, :, :, cols], sems.at[c]))
        copies[-1].start()
    for c in range(chunks):
        copies[c].wait()
        pack_columns(lambda k, n, at: held_ref[k, n, :, at], variables, inst, out_ref, c * width, width)


def pack_state(state, variables, chunks=2):
    inst, _, rows, cells = state.shape
    n = len(variables)
    return pl.pallas_call(
        functools.partial(pack_state_kernel, variables),
        in_specs=[IN_HBM],
        out_specs=IN_VMEM,
        out_shape=pltpu.VMEM((n, inst * rows, cells), jnp.bfloat16),
        scratch_shapes=[pltpu.VMEM((inst, n, rows, cells), jnp.float32), pltpu.SemaphoreType.DMA((chunks,))],
        compiler_params=params(4),
        name="pack_state",
    )(state)


def pack_more_kernel(variables, state_ref, out_ref):
    inst, _, _, cells = state_ref.shape
    pack_columns(lambda k, n, at: state_ref[k, variables[n], :, at], variables, inst, out_ref, 0, cells)


def pack_more(state, variables):
    inst, _, rows, cells = state.shape
    return pl.pallas_call(
        functools.partial(pack_more_kernel, variables),
        in_specs=[IN_VMEM],
        out_specs=IN_VMEM,
        out_shape=pltpu.VMEM((len(variables), inst * rows, cells), jnp.bfloat16),
        compiler_params=params(2),
        name="pack_more",
    )(state)


def pack_edges_kernel(state_ref, held_ref, first_ref, second_ref, sems):
    inst, nvar, rows, cells = state_ref.shape
    chunks = sems.shape[0]
    width = cells // chunks
    odd = lax.axis_index("brick") % 2 == 1
    copies = []
    for c in range(chunks):
        cols = pl.ds(c * width, width)
        copies.append(pltpu.make_async_copy(state_ref.at[:, :, :, cols], held_ref.at[:, :, :, cols], sems.at[c]))
        copies[-1].start()
    pair = lax.broadcasted_iota(jnp.int32, (rows, LANES), 0) // 2
    for c in range(chunks):
        copies[c].wait()

        def body(cols, _, base=c * width):
            at = pl.ds(pl.multiple_of(base + cols.start, LANES), LANES)
            for v in range(nvar):
                q = [held_ref[j, v, :, at] for j in range(inst)]
                head, tail = q[0], pltpu.roll(q[0], 2, 0)
                for j in range(1, inst):
                    head = jnp.where(pair == j, pltpu.roll(q[j], 2 * j, 0), head)
                    tail = jnp.where(pair == j, pltpu.roll(q[j], (2 * j + 2) % rows, 0) if (2 * j + 2) % rows else q[j], tail)
                first_ref[v, :, at] = jnp.where(odd, head, tail).astype(jnp.bfloat16)
                second_ref[v, :, at] = jnp.where(odd, tail, head).astype(jnp.bfloat16)

        columns(width, LANES, body)


def pack_edges(state, chunks=4):
    _, nvar, rows, cells = state.shape
    edge = pltpu.VMEM((nvar, rows, cells), jnp.bfloat16)
    return pl.pallas_call(
        pack_edges_kernel,
        in_specs=[IN_HBM],
        out_specs=[IN_VMEM] * 3,
        out_shape=[pltpu.VMEM(state.shape, jnp.float32), edge, edge],
        scratch_shapes=[pltpu.SemaphoreType.DMA((chunks,))],
        compiler_params=params(4),
        name="pack_edges",
    )(state)


def laid_out(group, cells):
    pieces, at = [], 0
    for v, lo, hi in group:
        count = (hi - lo) * cells // PARTS
        pieces.append((v, lo * cells // PARTS, count, at))
        at += count
    return pieces, at


def send_sums_kernel(base, period, state_ref, mate_ref, *out_refs):
    inst, _, _, cells = state_ref.shape
    parity = lax.axis_index("inst") % 2
    coefs = [row_coefs(j, inst, period, base, parity) for j in range(inst)]
    for group, out_ref in zip(SUM_GROUPS, out_refs):
        for v, first, count, to in laid_out(group, cells)[0]:

            def body(cols, _, v=v, first=first, to=to, out_ref=out_ref):
                for piece in range(UNROLL):
                    start = cols.start + piece * LANES
                    src = pl.ds(pl.multiple_of(first + start, LANES), LANES)
                    dst = pl.ds(pl.multiple_of(to + start, LANES), LANES)
                    values = [centred(ref[k, v, :, src], v) for ref in (state_ref, mate_ref) for k in range(inst)]
                    sums = [weighted(coefs[j], values) for j in range(inst)]
                    out_ref[:, dst] = jnp.concatenate(sums, axis=0).astype(jnp.bfloat16)

            columns(count, UNROLL * LANES, body)


def send_sums(state, mate, base, period):
    inst, _, rows, cells = state.shape
    return pl.pallas_call(
        functools.partial(send_sums_kernel, base, period),
        in_specs=[IN_VMEM] * 2,
        out_specs=[IN_VMEM] * len(SUM_GROUPS),
        out_shape=[pltpu.VMEM((inst * rows, laid_out(g, cells)[1]), jnp.bfloat16) for g in SUM_GROUPS],
        compiler_params=params(4),
        name="send_sums",
    )(state, mate)


def padded_size(size):
    return -(-size // LANES) * LANES


def cut_kernel(state_ref, blocks_ref, index_ref, type_ref, count_ref, back_ref, tiles_ref, wide_ref, lhs_ref):
    inst, nvar, rows, cells = state_ref.shape
    kinds, size, _ = blocks_ref.shape
    slots = index_ref.shape[1]
    per_row = cells // TILE
    wide = padded_size(size)
    half = cells // LANES * rows
    left = lax.broadcasted_iota(jnp.int32, (2 * rows, LANES), 1) < TILE

    full = size // LANES * LANES
    for kind in range(kinds):
        wide_ref[0:size, kind * wide:kind * wide + full] = blocks_ref[kind, :, 0:full]
        rest = blocks_ref[kind, :, full:size]
        if size > full:
            blank = jnp.zeros((size, wide - size), jnp.bfloat16)
            wide_ref[0:size, kind * wide + full:(kind + 1) * wide] = jnp.concatenate([rest, blank], axis=1)
    if wide > size:
        wide_ref[size:wide, :] = jnp.zeros((wide - size, kinds * wide), jnp.bfloat16)

    def gather(cols, c):
        for i in range(inst):
            q = []
            for v in range(nvar):
                pair = [state_ref[i, v, :, pl.ds(pl.multiple_of(cols.start + n * LANES, LANES), LANES)] for n in range(2)]
                q.append(jnp.concatenate(pair, axis=0))
            turned = [pltpu.roll(x, TILE, 1) for x in q]
            for p in range(wide // LANES):
                u, w = 2 * p, 2 * p + 1
                lo = jnp.where(left, q[u], turned[w] if w < nvar else 0.0)
                hi = jnp.where(left, turned[u], q[w] if w < nvar else 0.0)
                at = pl.ds(i * wide + p * LANES, LANES)
                row = pl.multiple_of(c * 2 * rows, 2 * rows)
                tiles_ref[pl.ds(row, 2 * rows), at] = lo.astype(jnp.bfloat16)
                tiles_ref[pl.ds(half + row, 2 * rows), at] = hi.astype(jnp.bfloat16)

    columns(cells, 2 * LANES, gather)

    index = index_ref[...]
    used = lax.broadcasted_iota(jnp.int32, (1, slots), 1) < count_ref[lax.axis_index("brick")]
    place = index % 2 * half + index % per_row // 2 * rows + index // per_row
    place = jnp.where(used, place, -1)
    code = jnp.where(used, type_ref[...] + 1, 0)
    both = jnp.concatenate([place, code, jnp.zeros((6, slots), jnp.int32)], axis=0).astype(jnp.float32)
    upright = jnp.transpose(both)
    place_of = upright[:, 0:1].astype(jnp.int32)
    code_of = jnp.broadcast_to(upright[:, 1:2], (slots, LANES)).astype(jnp.bfloat16)
    pick = jnp.where(lax.broadcasted_iota(jnp.int32, (slots, 2 * half), 1) == place_of, 1.0, 0.0).astype(jnp.bfloat16)
    give = jnp.where(lax.broadcasted_iota(jnp.int32, (2 * half, slots), 0) == place, 1.0, 0.0).astype(jnp.bfloat16)

    chosen = jnp.dot(pick, tiles_ref[...], preferred_element_type=jnp.float32).astype(jnp.bfloat16)
    for kind in range(kinds):
        keep = code_of == jnp.bfloat16(kind + 1.0)
        for i in range(inst):
            for p in range(wide // LANES):
                piece = chosen[:, i * wide + p * LANES:i * wide + (p + 1) * LANES]
                at = pl.ds(kind * wide + p * LANES, LANES)
                lhs_ref[pl.ds(i * slots, slots), at] = jnp.where(keep, piece, jnp.bfloat16(0.0))
    prod = lax.dot_general(
        lhs_ref[...], wide_ref[...], (((1,), (1,)), ((), ())), preferred_element_type=jnp.float32
    )
    high = prod.astype(jnp.bfloat16)
    low = (prod - high.astype(jnp.float32)).astype(jnp.bfloat16)
    for i in range(inst):
        at = pl.ds(i * wide, wide)
        tiles_ref[0:slots, at] = high[i * slots:(i + 1) * slots]
        tiles_ref[slots:2 * slots, at] = low[i * slots:(i + 1) * slots]
    give = jnp.concatenate([give, give], axis=1)
    back_ref[...] = jnp.dot(give, tiles_ref[0:2 * slots, :], preferred_element_type=jnp.float32)


def cut_terms(state, blocks, index, types, counts):
    inst, _, rows, cells = state.shape
    kinds, size, _ = blocks.shape
    slots = index.shape[1]
    wide = padded_size(size)
    tiles = cells // TILE * rows
    return pl.pallas_call(
        cut_kernel,
        in_specs=[IN_VMEM] * 4 + [IN_SMEM],
        out_specs=IN_VMEM,
        out_shape=pltpu.VMEM((tiles, inst * wide), jnp.float32),
        scratch_shapes=[
            pltpu.VMEM((max(tiles, 2 * slots), inst * wide), jnp.bfloat16),
            pltpu.VMEM((wide, kinds * wide), jnp.bfloat16),
            pltpu.VMEM((inst * slots, kinds * wide), jnp.bfloat16),
        ],
        compiler_params=params(24),
        name="cut_terms",
    )(state, blocks, index, types, counts)


def flux_of(q):
    inv = 1.0 / jnp.where(q[0] == 0.0, 1.0, q[0])
    speed = q[1] * inv
    press = GAMMA_MINUS * (q[4] - 0.5 * (q[1] * q[1] + q[2] * q[2] + q[3] * q[3]) * inv)
    return [q[1], q[1] * speed + press, q[2] * speed, q[3] * speed, (q[4] + press) * speed]


def stencil_kernel(period, state_ref, mate_ref, cut_ref, first_ref, second_ref, out_ref):
    inst, nvar, rows, cells = state_ref.shape
    parity = lax.axis_index("inst") % 2
    odd = lax.axis_index("brick") % 2 == 1
    coefs = [row_coefs(j, inst, period, 0, parity) for j in range(inst)]
    shares = [sum(c) for c in coefs]
    row = lax.broadcasted_iota(jnp.int32, (rows, LANES), 0)
    left = lax.broadcasted_iota(jnp.int32, (rows, LANES), 1) < TILE
    half, wide = cut_ref.shape[0] // 2, cut_ref.shape[1] // inst

    def body(cols, c):
        above, below = [], []
        at = pl.multiple_of(c * rows, rows)
        for v in range(nvar):
            first = first_ref[v, :, cols].astype(jnp.float32)
            second = second_ref[v, :, cols].astype(jnp.float32)
            above.append(jnp.where(odd, second, first))
            below.append(jnp.where(odd, first, second))
        for j in range(inst):
            up, down, smooth = [], [], []
            for v in range(nvar):
                x = state_ref[j, v, :, cols]
                h = jnp.where(row < rows // 2, turn(above[v], -2 * j), turn(below[v], rows - 2 - 2 * j))
                one = turn(jnp.where(row < 1, h, x), -1)
                two = turn(jnp.where(row < 2, h, x), -2)
                back = turn(jnp.where(row >= rows - 1, h, x), 1)
                back2 = turn(jnp.where(row >= rows - 2, h, x), 2)
                up.append(one)
                down.append(back)
                smooth.append(EPS_FOURTH * ((two + back2) - 4.0 * (one + back) + 6.0 * x))
            fup, fdown = flux_of(up), flux_of(down)
            for v in range(nvar):
                values = [ref[k, v, :, cols] for ref in (state_ref, mate_ref) for k in range(inst)]
                times = weighted(coefs[j], values)
                if CENTRE[v]:
                    times = times - CENTRE[v] * shares[j]
                total = 0.5 * (fup[v] - fdown[v]) + smooth[v] + times
                lanes = pl.ds(j * wide + v // 2 * LANES, LANES)
                lo, hi = cut_ref[pl.ds(at, rows), lanes], cut_ref[pl.ds(half + at, rows), lanes]
                if v % 2 == 0:
                    hi = pltpu.roll(hi, TILE, 1)
                else:
                    lo = pltpu.roll(lo, TILE, 1)
                out_ref[j, v, :, cols] = total + jnp.where(left, lo, hi)

    columns(cells, LANES, body)


def stencil(state, mate, cut, first, second, period):
    return pl.pallas_call(
        functools.partial(stencil_kernel, period),
        in_specs=[IN_VMEM] * 5,
        out_specs=IN_VMEM,
        out_shape=pltpu.VMEM(state.shape, jnp.float32),
        compiler_params=params(4),
        name="stencil",
    )(state, mate, cut, first, second)


def finish_kernel(groups, period, part_ref, state_ref, step_ref, *refs):
    inst, _, rows, _ = state_ref.shape
    res_ref, new_ref, res_held, new_held, sems = refs[-5:]
    parity = lax.axis_index("inst") % 2
    jobs, at = [], 0
    for whole, pieces, count in groups:
        got_refs = refs[at:at + count]
        at += count
        jobs += [(whole, n, v, first, size, to, got_refs) for n, (v, first, size, to) in enumerate(pieces)]
    copies = []
    for m, (whole, n, v, first, size, to, got_refs) in enumerate(jobs):

        def one_column(start, m=m, whole=whole, n=n, v=v, first=first, to=to, got_refs=got_refs):
            at = pl.ds(pl.multiple_of(first + start, LANES), LANES)
            dst = pl.ds(pl.multiple_of(to + start, LANES), LANES)
            totals = [part_ref[j, v, :, at] for j in range(inst)]
            if whole:
                for q in range(len(got_refs) // 2):
                    coefs = [row_coefs(j, inst, period, 2 * (q + 1), parity) for j in range(inst)]
                    rows_of = [ref[n, :, at].astype(jnp.float32) for ref in got_refs[2 * q:2 * q + 2]]
                    values = [x[k * rows:(k + 1) * rows] for x in rows_of for k in range(inst)]
                    totals = [t + weighted(cf, values) for t, cf in zip(totals, coefs)]
            else:
                for ref in got_refs:
                    g = ref[:, dst].astype(jnp.float32)
                    totals = [t + g[j * rows:(j + 1) * rows] for j, t in enumerate(totals)]
            for j in range(inst):
                res_held[j, m, :, at] = totals[j]
                new_held[j, m, :, at] = state_ref[j, v, :, at] - step_ref[:, at] * totals[j]

        chunks = sems.shape[2]
        width = size // chunks
        for c in range(chunks):

            def body(cols, _, base=c * width, one_column=one_column):
                for piece in range(UNROLL):
                    one_column(base + cols.start + piece * LANES)

            columns(width, UNROLL * LANES, body)
            cols = pl.ds(first + c * width, width)
            for held, out, which in ((res_held, res_ref, 0), (new_held, new_ref, 1)):
                copies.append(
                    pltpu.make_async_copy(held.at[:, m, :, cols], out.at[:, v, :, cols], sems.at[which, m, c])
                )
                copies[-1].start()
    for copy in copies:
        copy.wait()


def finish(groups, part, state, step, outs, period, chunks=2):
    inst, _, rows, cells = state.shape
    n = sum(len(pieces) for _, pieces, _ in groups)
    operands = [part, state, step] + [x for _, _, got in groups for x in got]
    specs = [IN_VMEM] * len(operands)
    aliases = {}
    if outs is not None:
        aliases = {len(operands): 0, len(operands) + 1: 1}
        operands += list(outs)
        specs += [IN_HBM] * 2
    return pl.pallas_call(
        functools.partial(finish_kernel, [(w, p, len(got)) for w, p, got in groups], period),
        in_specs=specs,
        out_specs=[IN_HBM] * 2,
        out_shape=[jax.ShapeDtypeStruct(state.shape, jnp.float32)] * 2,
        scratch_shapes=[
            pltpu.VMEM((inst, n, rows, cells), jnp.float32),
            pltpu.VMEM((inst, n, rows, cells), jnp.float32),
            pltpu.SemaphoreType.DMA((2, n, chunks)),
        ],
        input_output_aliases=aliases,
        compiler_params=params(8),
        name="finish",
    )(*operands)


def section(state, time_step, blocks, cut_counts, tile_index, tile_type):
    inst = state.shape[0]
    groups = lax.axis_size("inst")
    bricks = lax.axis_size("brick")
    period = inst * groups
    swap = [(i, i ^ 1) for i in range(groups)]
    hops = [[(i, (i + 2 * q) % groups) for i in range(groups)] for q in range(1, groups // 2)]
    cells = state.shape[3]
    state = pltpu.with_memory_space_constraint(state, pltpu.HBM)
    packed = [pack_state(state, STATE_GROUPS[0])]
    held, first, second = pack_edges(state)
    packed += [pack_more(held, group) for group in STATE_GROUPS[1:]]
    got_state = [[lax.ppermute(p, "inst", hop) for hop in hops] for p in packed]
    mate = pltpu.with_memory_space_constraint(lax.ppermute(held, "inst", swap), pltpu.VMEM)
    evens = [(b, b + 1) for b in range(0, bricks - 1, 2)]
    odds = [(b, b + 1) for b in range(1, bricks - 1, 2)]
    first = lax.ppermute(first, "brick", evens + [(b, a) for a, b in evens])
    second = lax.ppermute(second, "brick", odds + [(b, a) for a, b in odds])
    got_sums = [[] for _ in SUM_GROUPS]
    for q, hop in enumerate(hops):
        for g, part in enumerate(send_sums(held, mate, 2 * (q + 1), period)):
            got_sums[g].append(lax.ppermute(part, "inst", hop))
    cut = cut_terms(held, blocks, tile_index, tile_type, cut_counts)
    part = stencil(held, mate, cut, first, second, period)
    groups = []
    for variables, got in zip(STATE_GROUPS, got_state):
        pairs = []
        for x in got:
            pairs += [x, lax.ppermute(x, "inst", swap)]
        groups.append((True, [(v, 0, cells, 0) for v in variables], pairs))
    steps = [groups]
    steps += [[(False, laid_out(group, cells)[0], got)] for group, got in zip(SUM_GROUPS, got_sums)]
    outs = None
    for step in steps:
        outs = finish(step, part, held, time_step, outs, period)
    return tuple(outs)


def solution(mesh):
    placed = (
        P(("group", "inst"), None, "brick", None),
        P(("group", "brick"), None),
        P(),
        P("group"),
        P(("group", "brick"), None),
        P(("group", "brick"), None),
    )
    return jax.shard_map(
        section,
        mesh=mesh,
        in_specs=placed,
        out_specs=(
            P(("group", "inst"), None, "brick", None),
            P(("group", "inst"), None, "brick", None),
        ),
        check_vma=False,
    )
```
